256 devices in a mesh: node: 2 (over z_lo), row: 128 (over x, z_hi, y, core).
Axes of the slice: x: 4, y: 4, z: 8 (z_hi: 4, z_lo: 2; z = z_hi * 2 + z_lo), core: 2. Of those that a mesh axis runs over, the one named last changes fastest.
Arguments:
- hamiltonian: float32 [256, 7, 128, 128], P('row'), may hold values from -0.09375 to 0.09375
- column_blocks: int32 [256, 7], P('row'), may hold values from 0 to 255, as said below
- start_basis: float32 [32768, 256], P('row'), may hold values from -48 to 48
- node_re: float32 [6], P('node'), may hold values from 1.5 to 2.5
- node_im: float32 [6], P('node'), may hold values from 0.5 to 1.5
- weight_re: float32 [6], P('node'), may hold values from 0.5 to 1.5
- weight_im: float32 [6], P('node'), may hold values from -1 to 1
- sweep_count: int32 [6], P('node'), may hold values from 1 to 2, as said below
Outputs:
- basis: float32 [32768, 256], P('row')
The draws below stay inside these ranges and needn't reach their ends.
Inputs may be any that keep to these rules, and one draw needn't show every extreme that they name: `column_blocks`: tile 0 of row block b lies in column block b, tile 1 in b - 2 and tile 2 in b + 2, taken cyclically modulo 256; every other tile lies within 2 blocks of b, cyclically. `sweep_count`: some node takes 1 sweep and some node takes 2.
All inputs are finite; a program needn't handle non-finite values.
Results may differ from the reference program's by a relative error of at most 0.00022.
Values sent between devices are 32-bit elements; how exact they have to be, the bound alone decides.
A program may use at most 64 MiB of HBM per device.

```python
import math
import jax
import jax.numpy as jnp
from jax import lax

TILE = 128
VECS = 256
BLOCK_NNZ = 7
REACH = 2
SWEEPS = 2
NS_ITERS = 2
NODES = 6
BLOCKS = 256
ROWS = 32768


def draw_column_blocks(key, part):
    positions = jnp.arange(BLOCKS, dtype=jnp.int32)
    extra = jax.random.randint(jax.random.fold_in(key, 11), (BLOCKS, BLOCK_NNZ - 3), -REACH, REACH + 1).astype(jnp.int32)
    fixed_part = jnp.broadcast_to(jnp.array([0, -REACH, REACH], jnp.int32), (BLOCKS, 3))
    offsets = jnp.concatenate([fixed_part, extra], axis=1)
    return ((positions[:, None] + offsets + BLOCKS) % BLOCKS).astype(jnp.int32)


def draw_start_basis(key, part):
    key_base = jax.random.fold_in(key, 21)
    key_cols = jax.random.fold_in(key, 22)
    positions = jnp.arange(ROWS, dtype=jnp.float32) / ROWS
    col_scale = jnp.exp(jax.random.uniform(key_cols, (VECS,), jnp.float32, 0.0, jnp.log(3.0)))
    base = jax.random.truncated_normal(key_base, -4.0, 4.0, (ROWS, VECS), jnp.float32)
    row_scale = jnp.exp(jnp.log(3.0) * positions)
    return (base * row_scale[:, None] * col_scale[None, :]).astype(jnp.float32)


def draw_sweep_count(key, part):
    counts = jax.random.randint(jax.random.fold_in(key, 31), (NODES,), 1, SWEEPS + 1).astype(jnp.int32)
    order = jax.random.permutation(jax.random.fold_in(key, 32), NODES)
    counts = counts.at[order[0]].set(1)
    counts = counts.at[order[1]].set(SWEEPS)
    return counts.astype(jnp.int32)


def steps_of(own_key, dims, cuts, smallest, top_value):
    level, own = 1.0, jax.random.fold_in(own_key, 6)
    for dim, parts in cuts:
        heights = jnp.exp(jax.random.uniform(jax.random.fold_in(own, dim), (parts,), jnp.float32, smallest / len(cuts), top_value / len(cuts)))
        level = level * jnp.repeat(heights, dims[dim] // parts).reshape([-1 if axis == dim else 1 for axis in range(len(dims))])
    return level


def noise(stream_key, dims, width, reach, shards=(), kind=jnp.bfloat16):
    result = jax.random.normal(stream_key, dims, jnp.float32) * width
    if len(shards) > 0:
        result = steps_of(stream_key, dims, shards, -0.22, 0.18) * result
    return jnp.clip(result, min=-reach, max=reach).astype(kind)


def setup_inputs(seed: int = 0) -> dict:
    key_list = jax.random.split(jax.random.key(seed), 9)
    return {
        "hamiltonian": noise(key_list[0], (BLOCKS, BLOCK_NNZ, TILE, TILE), (4 * BLOCK_NNZ * TILE) ** -0.5, 0.09375, ((0, 128),), jnp.float32),
        "column_blocks": draw_column_blocks(jax.random.fold_in(key_list[8], 71), 0),
        "start_basis": draw_start_basis(jax.random.fold_in(key_list[8], 71), 0),
        "node_re": jnp.clip(1.5 + 1.0 * jax.random.uniform(key_list[3], (NODES,), jnp.float32) ** steps_of(key_list[3], (NODES,), ((0, 2),), -0.2, 0.2), 1.5, 2.5),
        "node_im": jnp.clip(0.5 + 1.0 * jax.random.uniform(key_list[4], (NODES,), jnp.float32) ** steps_of(key_list[4], (NODES,), ((0, 2),), -0.2, 0.2), 0.5, 1.5),
        "weight_re": jnp.clip(0.5 + 1.0 * jax.random.uniform(key_list[5], (NODES,), jnp.float32) ** steps_of(key_list[5], (NODES,), ((0, 2),), -0.2, 0.2), 0.5, 1.5),
        "weight_im": jnp.clip(jax.random.uniform(key_list[6], (NODES,), jnp.float32, -1.0, 1.0) * steps_of(key_list[6], (NODES,), ((0, 2),), -0.4, 0.0), -1.0, 1.0),
        "sweep_count": draw_sweep_count(jax.random.fold_in(key_list[8], 71), 0),
    }


def apply_tiles(hamiltonian, column_blocks, vectors):
    breadth = vectors.shape[1]
    blocks = vectors.reshape(BLOCKS, TILE, breadth)
    summed = jnp.zeros((BLOCKS, TILE, breadth), jnp.float32)
    for column in range(BLOCK_NNZ):
        picked = jnp.take(blocks, column_blocks[:, column].astype(jnp.int32), axis=0)
        summed = summed + jnp.einsum('bij,bjw->biw', hamiltonian[:, column], picked, precision=lax.Precision.HIGHEST)
    return summed.reshape(BLOCKS * TILE, breadth)

def orthonormal(gram_matrix):
    norm_value = jnp.sqrt(jnp.sum(gram_matrix * gram_matrix) + 1e-06)
    matrix_a = gram_matrix / norm_value
    identity = jnp.eye(gram_matrix.shape[0], dtype=jnp.float32)
    current = identity
    for repeat in range(NS_ITERS):
        middle = 1.5 * identity - 0.5 * jnp.dot(current, matrix_a, precision=lax.Precision.HIGHEST)
        matrix_a = jnp.dot(matrix_a, middle, precision=lax.Precision.HIGHEST)
        current = jnp.dot(middle, current, precision=lax.Precision.HIGHEST)
    return (current, norm_value)

def reference(hamiltonian, column_blocks, start_basis, node_re, node_im, weight_re, weight_im, sweep_count):
    modulus = node_re * node_re + node_im * node_im
    inverse_re = node_re / modulus
    inverse_im = -node_im / modulus
    power_re, power_im = (inverse_re, inverse_im)
    krylov = start_basis
    filtered = jnp.zeros_like(start_basis)
    for degree in range(SWEEPS + 1):
        if degree > 0:
            krylov = apply_tiles(hamiltonian, column_blocks, krylov)
        active = (sweep_count >= degree).astype(jnp.float32)
        weight_sum = jnp.sum(active * (weight_re * power_re - weight_im * power_im))
        filtered = filtered + weight_sum * krylov
        power_re, power_im = (power_re * inverse_re - power_im * inverse_im, power_re * inverse_im + power_im * inverse_re)
    gram_matrix = lax.dot_general(filtered, filtered, (((0,), (0,)), ((), ())), precision=lax.Precision.HIGHEST)
    mixing, norm_value = orthonormal(gram_matrix)
    return math.sqrt(ROWS) * jnp.dot(filtered, mixing, precision=lax.Precision.HIGHEST) / jnp.sqrt(norm_value)
```

```python
import functools
import itertools
import math

import jax
import jax.numpy as jnp
from jax import lax
from jax.experimental import pallas as pl
from jax.experimental.pallas import tpu as pltpu
from jax.sharding import Mesh
from jax.sharding import PartitionSpec as P

TILE = 128
REACH = 2
SWEEPS = 2
AXES = ("node", "x", "zh", "y", "core")
ROW = AXES[1:]
MESH = pl.DeviceIdType.MESH
F32 = jnp.float32
BF16 = jnp.bfloat16


def split(value):
    high = value.astype(BF16)
    return high, (value - high.astype(F32)).astype(BF16)


def product(left, right, dims=((1,), (0,))):
    def one(a, b):
        return lax.dot_general(a, b, (dims, ((), ())), preferred_element_type=F32)

    return one(left[0], right[0]) + (one(left[0], right[1]) + one(left[1], right[0]))


def pairwise(values):
    count = len(values)
    if count == 1:
        return values[0]
    if count == 2:
        return values[0] + values[1]
    return (values[0] + values[2]) + (values[1] + values[3])


def kernel(
    sizes,
    ham,
    cols,
    start,
    node_re,
    node_im,
    weight_re,
    weight_im,
    sweeps,
    out,
    ham_v,
    own,
    halo,
    krylov,
    halo1,
    band_hi,
    band_lo,
    coef,
    coef_in,
    part,
    rs_in,
    y_out,
    y_in,
    z_out,
    z_in,
    full,
    local_sem,
    halo_send,
    halo_recv,
    halo1_send,
    halo1_recv,
    coef_sem,
    rs_send,
    rs_recv,
    y_send,
    y_recv,
    z_send,
    z_recv,
    ag_send,
    ag_recv,
):
    nodes, nx, nzh, ny, cores = (sizes[a] for a in AXES)
    rows, width = start.shape
    piece = full.shape[0] // (nodes * nx * cores)
    me = {a: lax.axis_index(a) for a in AXES}
    ring = nx * nzh * ny * cores

    def away(**by):
        return {a: lax.rem(me[a] + by.get(a, 0) + sizes[a], sizes[a]) for a in AXES}

    position = ((me["x"] * nzh + me["zh"]) * ny + me["y"]) * cores + me["core"]

    def on_ring(step):
        at = lax.rem(position + step + ring, ring)
        return {
            "node": me["node"],
            "x": at // (nzh * ny * cores),
            "zh": lax.rem(at // (ny * cores), nzh),
            "y": lax.rem(at // cores, ny),
            "core": lax.rem(at, cores),
        }

    right, left = on_ring(1), on_ring(-1)

    ham_copy = pltpu.make_async_copy(ham, ham_v, local_sem.at[0])
    own_copy = pltpu.make_async_copy(start, own, local_sem.at[1])
    ham_copy.start()
    own_copy.start()

    rs_steps = [
        (dx, dc) for dx, dc in itertools.product(range(nx), range(cores)) if dx or dc
    ]
    ag_steps = [
        (dn, dx, dc)
        for dn, dx, dc in itertools.product(range(nodes), range(nx), range(cores))
        if dn or dx or dc
    ]
    peers = [left, right]
    peers += [away(node=dn, x=dx, core=dc) for dn, dx, dc in ag_steps]
    peers += [away(y=d) for d in range(1, ny)]
    peers += [away(zh=d) for d in range(1, nzh)]
    barrier = pltpu.get_barrier_semaphore()
    for peer in peers:
        pl.semaphore_signal(barrier, inc=1, device_id=peer, device_id_type=MESH)
    pl.semaphore_wait(barrier, len(peers))

    sent = []

    def send(src, dst, send_sem, recv_sem, peer):
        copy = pltpu.make_async_remote_copy(
            src_ref=src,
            dst_ref=dst,
            send_sem=send_sem,
            recv_sem=recv_sem,
            device_id=peer,
            device_id_type=MESH,
        )
        copy.start()
        sent.append(copy)
        return copy

    to_right = send(start, halo.at[0], halo_send.at[0], halo_recv.at[0], right)
    to_left = send(start, halo.at[1], halo_send.at[1], halo_recv.at[1], left)

    listed = [jnp.zeros((8, 128), F32) for _ in range(SWEEPS + 1)]
    for j in range(node_re.shape[0]):
        re, im = jnp.full((8, 128), node_re[j]), jnp.full((8, 128), node_im[j])
        w_re, w_im = jnp.full((8, 128), weight_re[j]), jnp.full((8, 128), weight_im[j])
        count = jnp.full((8, 128), sweeps[j])
        modulus = re * re + im * im
        inverse_re, inverse_im = re / modulus, -im / modulus
        power_re, power_im = inverse_re, inverse_im
        for degree in range(SWEEPS + 1):
            term = w_re * power_re - w_im * power_im
            listed[degree] = listed[degree] + jnp.where(count >= degree, term, 0.0)
            power_re, power_im = (
                power_re * inverse_re - power_im * inverse_im,
                power_re * inverse_im + power_im * inverse_re,
            )
    for degree, value in enumerate(listed):
        coef[8 * degree : 8 * degree + 8, :] = value
    coef_copy = send(coef, coef_in, coef_sem.at[0], coef_sem.at[1], away(node=1))

    ham_copy.wait()
    mine = rows // TILE
    blocks = mine * ring
    for a in range(mine):
        at = position * mine + a
        offset = [
            lax.rem(cols[a, k] - at + REACH + blocks, blocks) for k in range(ham.shape[1])
        ]
        for p in range(3 * mine):
            o = p - a + REACH - mine
            total = jnp.zeros((TILE, TILE), F32)
            if 0 <= o <= 2 * REACH:
                for k in range(ham.shape[1]):
                    fixed = (REACH, 0, 2 * REACH)
                    if k < 3:
                        if fixed[k] == o:
                            total = total + ham_v[a, k]
                    else:
                        total = total + jnp.where(offset[k] == o, 1.0, 0.0) * ham_v[a, k]
            high, low = split(total)
            place = (slice(a * TILE, (a + 1) * TILE), slice(p * TILE, (p + 1) * TILE))
            band_hi[place] = high
            band_lo[place] = low

    def band(side):
        at = slice(side * rows, (side + 1) * rows)
        return band_hi[:, at], band_lo[:, at]

    own_copy.wait()
    total = product(band(1), split(own[...]))
    to_right.wait_recv()
    total = total + product(band(0), split(halo[0]))
    to_left.wait_recv()
    total = total + product(band(2), split(halo[1]))
    krylov[...] = total
    to_right1 = send(krylov, halo1.at[0], halo1_send.at[0], halo1_recv.at[0], right)
    to_left1 = send(krylov, halo1.at[1], halo1_send.at[1], halo1_recv.at[1], left)
    coef_copy.wait_recv()
    scale = [
        (coef[8 * d : 8 * d + 8, :] + coef_in[8 * d : 8 * d + 8, :])[0:1, 0:1]
        for d in range(SWEEPS + 1)
    ]
    filtered = scale[0] * own[...] + scale[1] * total
    total = product(band(1), split(total))
    to_right1.wait_recv()
    total = total + product(band(0), split(halo1[0]))
    to_left1.wait_recv()
    total = total + product(band(2), split(halo1[1]))
    filtered = filtered + scale[2] * total

    f_split = split(filtered)
    half = width // 2
    first = tuple(v[:, :half] for v in f_split)
    last = tuple(v[:, half:] for v in f_split)
    top = product(first, f_split, ((0,), (0,)))
    part[0:half, :] = top[:, :half]
    part[half : 2 * half, :] = top[:, half:]
    part[2 * half :, :] = product(last, last, ((0,), (0,)))

    def piece_of(n, x, c):
        index = (n * nx + x) * cores + c
        return pl.ds(pl.multiple_of(index * piece, 8), piece)

    arriving = []
    for slot, (dx, dc) in enumerate(rs_steps):
        peer = away(x=dx, core=dc)
        theirs = piece_of(me["node"], peer["x"], peer["core"])
        arriving.append(
            send(part.at[theirs], rs_in.at[slot], rs_send.at[slot], rs_recv.at[slot], peer)
        )
    ours = piece_of(me["node"], me["x"], me["core"])
    value = part[ours, :]
    for slot, copy in enumerate(arriving):
        copy.wait_recv()
        value = value + rs_in[slot]

    def everywhere(value, axis, source, landing, send_sem, recv_sem):
        size = sizes[axis]
        if size == 1:
            return value
        source[...] = value
        copies = [
            send(source, landing.at[d - 1], send_sem.at[d - 1], recv_sem.at[d - 1], away(**{axis: d}))
            for d in range(1, size)
        ]
        for copy in copies:
            copy.wait_recv()
        return pairwise([value] + [landing[d - 1] for d in range(1, size)])

    value = everywhere(value, "y", y_out, y_in, y_send, y_recv)
    value = everywhere(value, "zh", z_out, z_in, z_send, z_recv)

    full[ours, :] = value
    for slot, (dn, dx, dc) in enumerate(ag_steps):
        send(full.at[ours], full.at[ours], ag_send.at[slot], ag_recv.at[slot], away(node=dn, x=dx, core=dc))
    for slot, (dn, dx, dc) in enumerate(ag_steps):
        source = away(node=-dn, x=-dx, core=-dc)
        theirs = piece_of(source["node"], source["x"], source["core"])
        pltpu.make_async_remote_copy(
            src_ref=full.at[theirs],
            dst_ref=full.at[theirs],
            send_sem=ag_send.at[slot],
            recv_sem=ag_recv.at[slot],
            device_id=source,
            device_id_type=MESH,
        ).wait_recv()

    corner = full[half : 2 * half, :]
    gram = jnp.concatenate(
        [
            jnp.concatenate([full[0:half, :], corner], axis=1),
            jnp.concatenate([corner.T, full[2 * half :, :]], axis=1),
        ],
        axis=0,
    )
    squares = jnp.sum(jnp.sum(gram * gram, axis=0, keepdims=True), axis=1, keepdims=True)
    norm = jnp.sqrt(squares + 1e-06)
    matrix = gram / norm
    m_split = split(matrix)
    square = product(m_split, m_split)
    mixed = product(split(square), split(0.0625 * square - 0.5625 * matrix))
    rows_at = lax.broadcasted_iota(jnp.int32, (width, width), 0)
    cols_at = lax.broadcasted_iota(jnp.int32, (width, width), 1)
    diagonal = jnp.where(rows_at == cols_at, 2.25, 0.0)
    mixed = mixed + (diagonal - 2.4375 * matrix + 1.6875 * square)
    result = product(f_split, split(mixed))
    out[...] = result * (math.sqrt(rows * ring) / jnp.sqrt(norm))

    for copy in sent:
        copy.wait_send()


def on_device(sizes, ham, cols, start, node_re, node_im, weight_re, weight_im, sweeps):
    rows, width = start.shape
    nodes, nx, nzh, ny, cores = (sizes[a] for a in AXES)
    packed = 3 * (width // 2)
    piece = packed // (nodes * nx * cores)
    anywhere = pl.BlockSpec(memory_space=pl.ANY)
    scalars = pl.BlockSpec(memory_space=pltpu.SMEM)
    vmem = pltpu.VMEM
    dma = pltpu.SemaphoreType.DMA
    others = nodes * nx * cores - 1
    near = nx * cores - 1
    return pl.pallas_call(
        functools.partial(kernel, sizes),
        out_shape=jax.ShapeDtypeStruct((rows, width), F32),
        in_specs=[anywhere, scalars, anywhere] + [scalars] * 5,
        out_specs=pl.BlockSpec(memory_space=pltpu.VMEM),
        scratch_shapes=[
            vmem(ham.shape, F32),
            vmem((rows, width), F32),
            vmem((2, rows, width), F32),
            vmem((rows, width), F32),
            vmem((2, rows, width), F32),
            vmem((rows, 3 * rows), BF16),
            vmem((rows, 3 * rows), BF16),
            vmem((8 * (SWEEPS + 1), 128), F32),
            vmem((8 * (SWEEPS + 1), 128), F32),
            vmem((packed, 128), F32),
            vmem((near, piece, 128), F32),
            vmem((piece, 128), F32),
            vmem((max(ny - 1, 1), piece, 128), F32),
            vmem((piece, 128), F32),
            vmem((max(nzh - 1, 1), piece, 128), F32),
            vmem((packed, 128), F32),
            dma((2,)),
            dma((2,)),
            dma((2,)),
            dma((2,)),
            dma((2,)),
            dma((2,)),
            dma((near,)),
            dma((near,)),
            dma((max(ny - 1, 1),)),
            dma((max(ny - 1, 1),)),
            dma((max(nzh - 1, 1),)),
            dma((max(nzh - 1, 1),)),
            dma((others,)),
            dma((others,)),
        ],
        compiler_params=pltpu.CompilerParams(
            collective_id=0, has_side_effects=True
        ),
    )(ham, cols, start, node_re, node_im, weight_re, weight_im, sweeps)


def build(finer):
    sizes = dict(finer.shape)
    return jax.shard_map(
        functools.partial(on_device, sizes),
        mesh=finer,
        in_specs=(
            P(ROW, None, None, None),
            P(ROW, None),
            P(ROW, None),
            P("node"),
            P("node"),
            P("node"),
            P("node"),
            P("node"),
        ),
        out_specs=P(ROW, None),
        check_vma=False,
    )


def solution(mesh):
    return build(Mesh(mesh.devices.reshape(mesh.shape["node"], 4, 4, 4, 2), AXES))
```

```python
import functools
import itertools
import math

import jax
import jax.numpy as jnp
from jax import lax
from jax.experimental import pallas as pl
from jax.experimental.pallas import tpu as pltpu
from jax.sharding import Mesh
from jax.sharding import PartitionSpec as P

TILE = 128
REACH = 2
SWEEPS = 2
AXES = ("node", "x", "zh", "y", "core")
ROW = AXES[1:]
MESH = pl.DeviceIdType.MESH
F32 = jnp.float32
BF16 = jnp.bfloat16


def split(value):
    high = value.astype(BF16)
    return high, (value - high.astype(F32)).astype(BF16)


def product(left, right, dims=((1,), (0,))):
    def one(a, b):
        return lax.dot_general(a, b, (dims, ((), ())), preferred_element_type=F32)

    return one(left[0], right[0]) + (one(left[0], right[1]) + one(left[1], right[0]))


def pairwise(values):
    count = len(values)
    if count == 1:
        return values[0]
    if count == 2:
        return values[0] + values[1]
    return (values[0] + values[2]) + (values[1] + values[3])


def steps_over(sizes, axes):
    found = itertools.product(*(range(sizes[a]) for a in axes))
    return [dict(zip(axes, by)) for by in found if any(by)]


class Sum:
    def __init__(self, net, refs):
        self.net = net
        (
            self.part, self.rs_in, self.y_out, self.y_in, self.z_out, self.z_in, self.full,
            self.rs_sem, self.y_sem, self.z_sem, self.ag_sem,
        ) = refs
        self.steps = steps_over(net.sizes, ("x", "core"))
        self.everyone = steps_over(net.sizes, ("node", "x", "core"))
        self.rows = self.y_out.shape[0]

    def piece(self, at):
        index = 0
        for axis in ("node", "x", "core"):
            index = index * self.net.sizes[axis] + at[axis]
        return pl.ds(pl.multiple_of(index * self.rows, 8), self.rows)

    def scatter(self):
        self.copies = [
            self.net.send(
                self.part.at[self.piece(self.net.away(**by))],
                self.rs_in.at[slot],
                self.rs_sem.at[0, slot],
                self.rs_sem.at[1, slot],
                self.net.away(**by),
            )
            for slot, by in enumerate(self.steps)
        ]

    def scattered(self):
        value = self.part[self.piece(self.net.me), :]
        for slot, copy in enumerate(self.copies):
            copy.wait_recv()
            value = value + self.rs_in[slot]
        return value

    def share(self, value, axis, source, landing, sem):
        source[...] = value
        self.value = value
        self.landing = landing
        self.copies = [
            self.net.send(source, landing.at[d - 1], sem.at[0, d - 1], sem.at[1, d - 1], self.net.away(**{axis: d}))
            for d in range(1, self.net.sizes[axis])
        ]

    def shared(self):
        for copy in self.copies:
            copy.wait_recv()
        return pairwise([self.value] + [self.landing[d] for d in range(len(self.copies))])

    def to_y(self):
        self.share(self.scattered(), "y", self.y_out, self.y_in, self.y_sem)

    def to_z(self):
        self.share(self.shared(), "zh", self.z_out, self.z_in, self.z_sem)

    def gather(self):
        value = self.shared()
        ours = self.piece(self.net.me)
        self.full[ours, :] = value
        for slot, by in enumerate(self.everyone):
            self.net.send(
                self.full.at[ours],
                self.full.at[ours],
                self.ag_sem.at[0, slot],
                self.ag_sem.at[1, slot],
                self.net.away(**by),
            )

    def gathered(self):
        for slot, by in enumerate(self.everyone):
            source = self.net.away(**{a: -d for a, d in by.items()})
            theirs = self.full.at[self.piece(source)]
            self.net.copy(
                theirs, theirs, self.ag_sem.at[0, slot], self.ag_sem.at[1, slot], source
            ).wait_recv()


class Net:
    def __init__(self, sizes):
        self.sizes = sizes
        self.me = {a: lax.axis_index(a) for a in AXES}
        self.sent = []
        self.ring = math.prod(sizes[a] for a in ROW)
        me = self.me
        self.position = (
            (me["x"] * sizes["zh"] + me["zh"]) * sizes["y"] + me["y"]
        ) * sizes["core"] + me["core"]

    def away(self, **by):
        return {
            a: lax.rem(self.me[a] + by[a] + self.sizes[a], self.sizes[a]) if by.get(a) else self.me[a]
            for a in AXES
        }

    def on_ring(self, step):
        at = lax.rem(self.position + step + self.ring, self.ring)
        zh, y, core = (self.sizes[a] for a in ("zh", "y", "core"))
        return {
            "node": self.me["node"],
            "x": at // (zh * y * core),
            "zh": lax.rem(at // (y * core), zh),
            "y": lax.rem(at // core, y),
            "core": lax.rem(at, core),
        }

    def copy(self, src, dst, send_sem, recv_sem, peer):
        return pltpu.make_async_remote_copy(
            src_ref=src,
            dst_ref=dst,
            send_sem=send_sem,
            recv_sem=recv_sem,
            device_id=peer,
            device_id_type=MESH,
        )

    def send(self, *what):
        copy = self.copy(*what)
        copy.start()
        self.sent.append(copy)
        return copy


class Halo:
    def __init__(self, net, halo, sem):
        self.net, self.halo, self.sem = net, halo, sem
        self.near = (0, net.sizes["node"] - 1)
        me, last = net.me, {a: net.sizes[a] - 1 for a in AXES}
        first_in_line = (me["y"] == 0) & (me["core"] == 0)
        last_in_line = (me["y"] == last["y"]) & (me["core"] == last["core"])
        self.receives = (first_in_line, last_in_line)
        self.sends = (last_in_line, first_in_line)
        self.tile = halo.shape[2] // 2

    def target(self, slot):
        peer = self.net.on_ring(1 if slot == 0 else -1)
        return {**peer, "node": jnp.where(self.sends[slot], self.near[slot], self.net.me["node"])}

    def sending(self, slot):
        return jnp.logical_not(self.sends[slot]) | (self.net.me["node"] != self.near[slot])

    def unit(self, slot, c, j):
        return self.halo.at[slot, c, j * self.tile : (j + 1) * self.tile, :]

    def direct(self, src, slot, c, j):
        return self.net.copy(
            src, self.unit(slot, c, j), self.sem.at[0, slot, c, j], self.sem.at[1, slot, c, j], self.target(slot)
        )

    def onward(self, slot, c, j):
        at = self.unit(slot, c, j)
        return self.net.copy(
            at, at, self.sem.at[2, slot, c, j], self.sem.at[1, slot, c, j], self.net.away(node=1)
        )

    def relaying(self, slot):
        return self.receives[slot] & (self.net.me["node"] == self.near[slot])

    def send(self, source, c):
        for slot in range(2):

            @pl.when(self.sending(slot))
            def _():
                for j in range(2):
                    self.direct(source(c, j), slot, c, j).start()

    def receive(self, c):
        for slot in range(2):
            for j in range(2):
                self.onward(slot, c, j).wait_recv()

                @pl.when(self.relaying(slot))
                def _():
                    self.onward(slot, c, j).start()

    def finish(self):
        for slot in range(2):
            for c, j in itertools.product(range(2), range(2)):

                @pl.when(self.sending(slot))
                def _():
                    self.direct(self.unit(slot, c, j), slot, c, j).wait_send()

                @pl.when(self.relaying(slot))
                def _():
                    self.onward(slot, c, j).wait_send()


def kernel(
    sizes,
    ham,
    cols,
    start,
    node_re,
    node_im,
    weight_re,
    weight_im,
    sweeps,
    out,
    ham_v,
    own,
    halo_v,
    krylov,
    halo1_v,
    band_hi,
    band_lo,
    coef,
    coef_in,
    local_sem,
    halo_sem,
    halo1_sem,
    coef_sem,
    *sums,
):
    rows, width = start.shape
    half = width // 2
    net = Net(sizes)
    me, send = net.me, net.send
    position, ring = net.position, net.ring
    twin = net.away(node=1)

    ham_copy = pltpu.make_async_copy(ham, ham_v, local_sem.at[0])
    own_copy = pltpu.make_async_copy(start, own, local_sem.at[1])
    ham_copy.start()
    own_copy.start()

    peers = [net.away(**by) for by in steps_over(sizes, ("node", "x", "core"))]
    peers += [net.away(y=d) for d in range(1, sizes["y"])]
    peers += [net.away(zh=d) for d in range(1, sizes["zh"])]
    for step in (-1, 1):
        at = net.on_ring(step)
        peers += [at, {**at, "node": twin["node"]}]
    barrier = pltpu.get_barrier_semaphore()
    for peer in peers:
        pl.semaphore_signal(barrier, inc=1, device_id=peer, device_id_type=MESH)
    pl.semaphore_wait(barrier, len(peers))

    first = Halo(net, halo_v, halo_sem)
    second = Halo(net, halo1_v, halo1_sem)

    def of_start(c, j):
        return start.at[j * TILE : (j + 1) * TILE, c * half : (c + 1) * half]

    def of_krylov(c, j):
        return krylov.at[c, j * TILE : (j + 1) * TILE, :]

    for c in range(2):
        first.send(of_start, c)

    listed = [jnp.zeros((8, 128), F32) for _ in range(SWEEPS + 1)]
    for j in range(node_re.shape[0]):
        re, im = jnp.full((8, 128), node_re[j]), jnp.full((8, 128), node_im[j])
        w_re, w_im = jnp.full((8, 128), weight_re[j]), jnp.full((8, 128), weight_im[j])
        count = jnp.full((8, 128), sweeps[j])
        modulus = re * re + im * im
        inverse_re, inverse_im = re / modulus, -im / modulus
        power_re, power_im = inverse_re, inverse_im
        for degree in range(SWEEPS + 1):
            term = w_re * power_re - w_im * power_im
            listed[degree] = listed[degree] + jnp.where(count >= degree, term, 0.0)
            power_re, power_im = (
                power_re * inverse_re - power_im * inverse_im,
                power_re * inverse_im + power_im * inverse_re,
            )
    for degree, value in enumerate(listed):
        coef[8 * degree : 8 * degree + 8, :] = value
    coef_copy = send(coef, coef_in, coef_sem.at[0], coef_sem.at[1], twin)

    ham_copy.wait()
    mine = rows // TILE
    blocks = mine * ring
    for a in range(mine):
        at = position * mine + a
        offset = [
            lax.rem(cols[a, k] - at + REACH + blocks, blocks) for k in range(ham.shape[1])
        ]
        for p in range(3 * mine):
            o = p - a + REACH - mine
            total = jnp.zeros((TILE, TILE), F32)
            if 0 <= o <= 2 * REACH:
                for k in range(ham.shape[1]):
                    fixed = (REACH, 0, 2 * REACH)
                    if k < 3:
                        if fixed[k] == o:
                            total = total + ham_v[a, k]
                    else:
                        total = total + jnp.where(offset[k] == o, 1.0, 0.0) * ham_v[a, k]
            high, low = split(total)
            place = (slice(a * TILE, (a + 1) * TILE), slice(p * TILE, (p + 1) * TILE))
            band_hi[place] = high
            band_lo[place] = low

    def band(side):
        at = slice(side * rows, (side + 1) * rows)
        return band_hi[:, at], band_lo[:, at]

    own_copy.wait()
    parts = []
    for c in range(2):
        parts.append(product(band(1), split(own[:, c * half : (c + 1) * half])))
    for c in range(2):
        first.receive(c)
        total = parts[c] + product(band(0), split(halo_v[0, c]))
        total = total + product(band(2), split(halo_v[1, c]))
        krylov[c] = total
        second.send(of_krylov, c)
    coef_copy.wait_recv()
    scale = [
        (coef[8 * d : 8 * d + 8, :] + coef_in[8 * d : 8 * d + 8, :])[0:1, 0:1]
        for d in range(SWEEPS + 1)
    ]
    filtered, parts = [], []
    for c in range(2):
        total = krylov[c]
        filtered.append(scale[0] * own[:, c * half : (c + 1) * half] + scale[1] * total)
        parts.append(product(band(1), split(total)))
    for c in range(2):
        second.receive(c)
        total = parts[c] + product(band(0), split(halo1_v[0, c]))
        total = total + product(band(2), split(halo1_v[1, c]))
        filtered[c] = split(filtered[c] + scale[2] * total)

    packed = Sum(net, sums)
    for k, (a, b) in enumerate(((0, 0), (0, 1), (1, 1))):
        packed.part[k * half : (k + 1) * half, :] = product(filtered[a], filtered[b], ((0,), (0,)))
    packed.scatter()
    packed.to_y()
    packed.to_z()
    packed.gather()
    f_split = tuple(jnp.concatenate(v, axis=1) for v in zip(*filtered))
    packed.gathered()

    corner = packed.full[half : 2 * half, :]
    gram = jnp.concatenate(
        [
            jnp.concatenate([packed.full[0:half, :], corner], axis=1),
            jnp.concatenate([corner.T, packed.full[2 * half :, :]], axis=1),
        ],
        axis=0,
    )
    squares = jnp.sum(jnp.sum(gram * gram, axis=0, keepdims=True), axis=1, keepdims=True)
    norm = jnp.sqrt(squares + 1e-06)
    matrix = gram / norm
    m_split = split(matrix)
    square = product(m_split, m_split)
    mixed = product(split(square), split(0.0625 * square - 0.5625 * matrix))
    rows_at = lax.broadcasted_iota(jnp.int32, (width, width), 0)
    cols_at = lax.broadcasted_iota(jnp.int32, (width, width), 1)
    diagonal = jnp.where(rows_at == cols_at, 2.25, 0.0)
    mixed = mixed + (diagonal - 2.4375 * matrix + 1.6875 * square)
    result = product(f_split, split(mixed))
    out[...] = result * (math.sqrt(rows * ring) / jnp.sqrt(norm))

    for copy in net.sent:
        copy.wait_send()
    first.finish()
    second.finish()


def on_device(sizes, ham, cols, start, node_re, node_im, weight_re, weight_im, sweeps):
    rows, width = start.shape
    half = width // 2
    anywhere = pl.BlockSpec(memory_space=pl.ANY)
    scalars = pl.BlockSpec(memory_space=pltpu.SMEM)
    vmem = pltpu.VMEM
    dma = pltpu.SemaphoreType.DMA
    y, zh = max(sizes["y"] - 1, 1), max(sizes["zh"] - 1, 1)
    everyone = sizes["node"] * sizes["x"] * sizes["core"]

    packed = 3 * half
    piece = packed // everyone
    near = sizes["x"] * sizes["core"] - 1
    return pl.pallas_call(
        functools.partial(kernel, sizes),
        out_shape=jax.ShapeDtypeStruct((rows, width), F32),
        in_specs=[anywhere, scalars, anywhere] + [scalars] * 5,
        out_specs=pl.BlockSpec(memory_space=pltpu.VMEM),
        scratch_shapes=[
            vmem(ham.shape, F32),
            vmem((rows, width), F32),
            vmem((2, 2, rows, half), F32),
            vmem((2, rows, half), F32),
            vmem((2, 2, rows, half), F32),
            vmem((rows, 3 * rows), BF16),
            vmem((rows, 3 * rows), BF16),
            vmem((8 * (SWEEPS + 1), 128), F32),
            vmem((8 * (SWEEPS + 1), 128), F32),
            dma((2,)),
            dma((3, 2, 2, 2)),
            dma((3, 2, 2, 2)),
            dma((2,)),
            vmem((packed, half), F32),
            vmem((near, piece, half), F32),
            vmem((piece, half), F32),
            vmem((y, piece, half), F32),
            vmem((piece, half), F32),
            vmem((zh, piece, half), F32),
            vmem((packed, half), F32),
            dma((2, near)),
            dma((2, y)),
            dma((2, zh)),
            dma((2, everyone - 1)),
        ],
        compiler_params=pltpu.CompilerParams(collective_id=0, has_side_effects=True),
    )(ham, cols, start, node_re, node_im, weight_re, weight_im, sweeps)


def build(finer):
    sizes = dict(finer.shape)
    return jax.shard_map(
        functools.partial(on_device, sizes),
        mesh=finer,
        in_specs=(
            P(ROW, None, None, None),
            P(ROW, None),
            P(ROW, None),
            P("node"),
            P("node"),
            P("node"),
            P("node"),
            P("node"),
        ),
        out_specs=P(ROW, None),
        check_vma=False,
    )


def solution(mesh):
    return build(Mesh(mesh.devices.reshape(mesh.shape["node"], 4, 4, 4, 2), AXES))
```

```python
import functools
import itertools
import math

import jax
import jax.numpy as jnp
from jax import lax
from jax.experimental import pallas as pl
from jax.experimental.pallas import tpu as pltpu
from jax.sharding import Mesh
from jax.sharding import PartitionSpec as P

TILE = 128
REACH = 2
SWEEPS = 2
AXES = ("node", "x", "zh", "y", "core")
ROW = AXES[1:]
MESH = pl.DeviceIdType.MESH
F32 = jnp.float32
BF16 = jnp.bfloat16


def split(value):
    high = value.astype(BF16)
    return high, (value - high.astype(F32)).astype(BF16)


def product(left, right, dims=((1,), (0,))):
    def one(a, b):
        return lax.dot_general(a, b, (dims, ((), ())), preferred_element_type=F32)

    return one(left[0], right[0]) + (one(left[0], right[1]) + one(left[1], right[0]))


def pairwise(values):
    count = len(values)
    if count == 1:
        return values[0]
    if count == 2:
        return values[0] + values[1]
    return (values[0] + values[2]) + (values[1] + values[3])


def steps_over(sizes, axes):
    found = itertools.product(*(range(sizes[a]) for a in axes))
    return [dict(zip(axes, by)) for by in found if any(by)]


class Sum:
    def __init__(self, net, refs):
        self.net = net
        (
            self.part, self.rs_in, self.y_out, self.y_in, self.z_out, self.z_in, self.full,
            self.rs_sem, self.y_sem, self.z_sem, self.ag_sem,
        ) = refs
        self.everyone = steps_over(net.sizes, ("node", "x", "core"))
        self.rows = self.y_out.shape[0]

    def piece(self, at):
        index = 0
        for axis in ("node", "x", "core"):
            index = index * self.net.sizes[axis] + at[axis]
        return pl.ds(pl.multiple_of(index * self.rows, 8), self.rows)

    def partial(self, slot, by):
        peer = self.net.away(**by)
        landing = by["x"] * self.net.sizes["core"] + by["core"]
        return self.net.copy(
            self.part.at[self.piece(peer)],
            self.rs_in.at[landing],
            self.rs_sem.at[0, slot],
            self.rs_sem.at[1, landing],
            peer,
        )

    def scattering(self, by):
        here = jnp.logical_not(self.net.far)
        return here if by["node"] == 0 else here & self.net.edge

    def scatter(self):
        for slot, by in enumerate(self.everyone):

            @pl.when(self.scattering(by))
            def _():
                self.partial(slot, by).start()

    def finish(self):
        for slot, by in enumerate(self.everyone):

            @pl.when(self.scattering(by))
            def _():
                self.partial(slot, by).wait_send()

    def scattered(self):
        ours = self.piece(self.net.me)

        def arrived(landing):
            at = self.rs_in.at[landing]
            self.net.copy(at, at, self.rs_sem.at[0, 0], self.rs_sem.at[1, landing], self.net.away(node=1)).wait_recv()

        @pl.when(self.net.far)
        def _():
            arrived(0)
            self.part[ours, :] = self.rs_in[0]

        value = self.part[ours, :]
        for landing in range(1, self.rs_in.shape[0]):
            arrived(landing)
            value = value + self.rs_in[landing]
        return value

    def share(self, value, axis, source, landing, sem):
        source[...] = value
        self.value = value
        self.landing = landing
        self.copies = [
            self.net.send(source, landing.at[d - 1], sem.at[0, d - 1], sem.at[1, d - 1], self.net.away(**{axis: d}))
            for d in range(1, self.net.sizes[axis])
        ]

    def shared(self):
        for copy in self.copies:
            copy.wait_recv()
        return pairwise([self.value] + [self.landing[d] for d in range(len(self.copies))])

    def to_y(self):
        self.share(self.scattered(), "y", self.y_out, self.y_in, self.y_sem)

    def to_z(self):
        self.share(self.shared(), "zh", self.z_out, self.z_in, self.z_sem)

    def gather(self):
        value = self.shared()
        ours = self.piece(self.net.me)
        self.full[ours, :] = value
        for slot, by in enumerate(self.everyone):
            self.net.send(
                self.full.at[ours],
                self.full.at[ours],
                self.ag_sem.at[0, slot],
                self.ag_sem.at[1, slot],
                self.net.away(**by),
            )

    def gathered(self):
        for slot, by in enumerate(self.everyone):
            source = self.net.away(**{a: -d for a, d in by.items()})
            theirs = self.full.at[self.piece(source)]
            self.net.copy(
                theirs, theirs, self.ag_sem.at[0, slot], self.ag_sem.at[1, slot], source
            ).wait_recv()


class Net:
    def __init__(self, sizes):
        self.sizes = sizes
        self.me = {a: lax.axis_index(a) for a in AXES}
        self.sent = []
        self.ring = math.prod(sizes[a] for a in ROW)
        me = self.me
        self.position = (
            (me["x"] * sizes["zh"] + me["zh"]) * sizes["y"] + me["y"]
        ) * sizes["core"] + me["core"]
        head = (me["y"] == 0) & (me["core"] == 0)
        tail = (me["y"] == sizes["y"] - 1) & (me["core"] == sizes["core"] - 1)
        self.receives, self.sends = (head, tail), (tail, head)
        self.near = (0, sizes["node"] - 1)
        self.edge = head | tail
        self.far = (head & (me["node"] != self.near[0])) | (tail & (me["node"] != self.near[1]))

    def sending(self, slot):
        return jnp.logical_not(self.sends[slot]) | (self.me["node"] != self.near[slot])

    def target(self, slot):
        node = jnp.where(self.sends[slot], self.near[slot], self.me["node"])
        return {**self.on_ring(1 if slot == 0 else -1), "node": node}

    def relaying(self, slot):
        return self.receives[slot] & (self.me["node"] == self.near[slot])

    def source(self, slot):
        node = jnp.where(self.receives[slot], self.sizes["node"] - 1 - self.near[slot], self.me["node"])
        return {**self.on_ring(-1 if slot == 0 else 1), "node": node}

    def sourced(self, slot):
        return jnp.logical_not(self.receives[slot]) | (self.me["node"] == self.near[slot])

    def away(self, **by):
        return {
            a: lax.rem(self.me[a] + by[a] + self.sizes[a], self.sizes[a]) if by.get(a) else self.me[a]
            for a in AXES
        }

    def on_ring(self, step):
        at = lax.rem(self.position + step + self.ring, self.ring)
        zh, y, core = (self.sizes[a] for a in ("zh", "y", "core"))
        return {
            "node": self.me["node"],
            "x": at // (zh * y * core),
            "zh": lax.rem(at // (y * core), zh),
            "y": lax.rem(at // core, y),
            "core": lax.rem(at, core),
        }

    def copy(self, src, dst, send_sem, recv_sem, peer):
        return pltpu.make_async_remote_copy(
            src_ref=src,
            dst_ref=dst,
            send_sem=send_sem,
            recv_sem=recv_sem,
            device_id=peer,
            device_id_type=MESH,
        )

    def send(self, *what):
        copy = self.copy(*what)
        copy.start()
        self.sent.append(copy)
        return copy


class Halo:
    def __init__(self, net, halo, sem):
        self.net, self.halo, self.sem = net, halo, sem
        self.tile = halo.shape[2] // 2

    def unit(self, slot, c, j):
        return self.halo.at[slot, c, j * self.tile : (j + 1) * self.tile, :]

    def direct(self, src, slot, c, j):
        return self.net.copy(
            src, self.unit(slot, c, j), self.sem.at[0, slot, c, j], self.sem.at[1, slot, c, j], self.net.target(slot)
        )

    def onward(self, slot, c, j):
        at = self.unit(slot, c, j)
        return self.net.copy(
            at, at, self.sem.at[2, slot, c, j], self.sem.at[1, slot, c, j], self.net.away(node=1)
        )

    def send(self, source, c):
        for slot in range(2):

            @pl.when(self.net.sending(slot))
            def _():
                for j in range(2):
                    self.direct(source(c, j), slot, c, j).start()

    def receive(self, c):
        for slot in range(2):
            for j in range(2):
                self.onward(slot, c, j).wait_recv()

                @pl.when(self.net.relaying(slot))
                def _():
                    self.onward(slot, c, j).start()

    def finish(self):
        for slot in range(2):
            for c, j in itertools.product(range(2), range(2)):

                @pl.when(self.net.sending(slot))
                def _():
                    self.direct(self.unit(slot, c, j), slot, c, j).wait_send()

                @pl.when(self.net.relaying(slot))
                def _():
                    self.onward(slot, c, j).wait_send()


def kernel(
    sizes,
    ham,
    cols,
    start,
    node_re,
    node_im,
    weight_re,
    weight_im,
    sweeps,
    out,
    ham_v,
    own,
    halo_v,
    krylov,
    halo1_v,
    band_hi,
    band_lo,
    coef,
    coef_in,
    filt_hi,
    filt_lo,
    local_sem,
    halo_sem,
    halo1_sem,
    coef_sem,
    told,
    *sums,
):
    rows, width = start.shape
    half = width // 2
    net = Net(sizes)
    me, send = net.me, net.send
    position, ring = net.position, net.ring
    twin = net.away(node=1)

    ham_copy = pltpu.make_async_copy(ham, ham_v, local_sem.at[0])
    own_copy = pltpu.make_async_copy(start, own, local_sem.at[1])
    ham_copy.start()
    own_copy.start()

    along = [net.away(**{a: d}) for a in ("x", "y", "zh") for d in sorted({1, sizes[a] - 1} - {0})]
    mate = net.away(core=1)
    peers = [mate, twin, *along]
    barrier = pltpu.get_barrier_semaphore()
    greeted = len(peers)
    for slot in range(2):

        @pl.when(net.sourced(slot))
        def _():
            pl.semaphore_signal(barrier, inc=1, device_id=net.source(slot), device_id_type=MESH)

        greeted = greeted + net.sending(slot).astype(jnp.int32)
    for peer in peers:
        pl.semaphore_signal(barrier, inc=1, device_id=peer, device_id_type=MESH)
    pl.semaphore_wait(barrier, greeted)

    rounds = (along, [mate, twin], [mate])

    def tell(at):
        for peer in rounds[at]:
            pl.semaphore_signal(told.at[at], inc=1, device_id=peer, device_id_type=MESH)

    def hear(at):
        if rounds[at]:
            pl.semaphore_wait(told.at[at], len(rounds[at]))


    first = Halo(net, halo_v, halo_sem)
    second = Halo(net, halo1_v, halo1_sem)

    def of_start(c, j):
        return start.at[j * TILE : (j + 1) * TILE, c * half : (c + 1) * half]

    def of_krylov(c, j):
        return krylov.at[c, j * TILE : (j + 1) * TILE, :]

    for c in range(2):
        first.send(of_start, c)
    tell(0)

    listed = [jnp.zeros((8, 128), F32) for _ in range(SWEEPS + 1)]
    for j in range(node_re.shape[0]):
        re, im = jnp.full((8, 128), node_re[j]), jnp.full((8, 128), node_im[j])
        w_re, w_im = jnp.full((8, 128), weight_re[j]), jnp.full((8, 128), weight_im[j])
        count = jnp.full((8, 128), sweeps[j])
        modulus = re * re + im * im
        inverse_re, inverse_im = re / modulus, -im / modulus
        power_re, power_im = inverse_re, inverse_im
        for degree in range(SWEEPS + 1):
            term = w_re * power_re - w_im * power_im
            listed[degree] = listed[degree] + jnp.where(count >= degree, term, 0.0)
            power_re, power_im = (
                power_re * inverse_re - power_im * inverse_im,
                power_re * inverse_im + power_im * inverse_re,
            )
    for degree, value in enumerate(listed):
        coef[8 * degree : 8 * degree + 8, :] = value
    coef_copy = send(coef, coef_in, coef_sem.at[0], coef_sem.at[1], twin)

    ham_copy.wait()
    mine = rows // TILE
    blocks = mine * ring
    for a in range(mine):
        at = position * mine + a
        offset = [
            lax.rem(cols[a, k] - at + REACH + blocks, blocks) for k in range(ham.shape[1])
        ]
        for p in range(3 * mine):
            o = p - a + REACH - mine
            total = jnp.zeros((TILE, TILE), F32)
            if 0 <= o <= 2 * REACH:
                for k in range(ham.shape[1]):
                    fixed = (REACH, 0, 2 * REACH)
                    if k < 3:
                        if fixed[k] == o:
                            total = total + ham_v[a, k]
                    else:
                        total = total + jnp.where(offset[k] == o, 1.0, 0.0) * ham_v[a, k]
            high, low = split(total)
            place = (slice(a * TILE, (a + 1) * TILE), slice(p * TILE, (p + 1) * TILE))
            band_hi[place] = high
            band_lo[place] = low

    def band(side):
        at = slice(side * rows, (side + 1) * rows)
        return band_hi[:, at], band_lo[:, at]

    own_copy.wait()
    parts = []
    for c in range(2):
        parts.append(product(band(1), split(own[:, c * half : (c + 1) * half])))
    for c in range(2):
        first.receive(c)
        total = parts[c] + product(band(0), split(halo_v[0, c]))
        total = total + product(band(2), split(halo_v[1, c]))
        krylov[c] = total
        second.send(of_krylov, c)
        hear(c)
        tell(c + 1)
    hear(2)
    coef_copy.wait_recv()
    scale = [
        (coef[8 * d : 8 * d + 8, :] + coef_in[8 * d : 8 * d + 8, :])[0:1, 0:1]
        for d in range(SWEEPS + 1)
    ]
    parts = [product(band(1), split(krylov[c])) for c in range(2)]
    packed = Sum(net, sums)

    def filter_rows():
        for c in range(2):
            second.receive(c)
            at = slice(c * half, (c + 1) * half)
            total = parts[c] + product(band(0), split(halo1_v[0, c]))
            total = total + product(band(2), split(halo1_v[1, c]))
            total = scale[0] * own[:, at] + scale[1] * krylov[c] + scale[2] * total
            filt_hi[:, at], filt_lo[:, at] = split(total)

    @pl.when(jnp.logical_not(net.far))
    def _():
        filter_rows()
        halves = [
            (filt_hi[:, c * half : (c + 1) * half], filt_lo[:, c * half : (c + 1) * half]) for c in range(2)
        ]
        for k, (a, b) in enumerate(((0, 0), (0, 1), (1, 1))):
            packed.part[k * half : (k + 1) * half, :] = product(halves[a], halves[b], ((0,), (0,)))
    packed.scatter()
    packed.to_y()
    packed.to_z()
    packed.gather()
    pl.when(net.far)(filter_rows)
    packed.gathered()
    f_split = (filt_hi[...], filt_lo[...])

    corner = packed.full[half : 2 * half, :]
    gram = jnp.concatenate(
        [
            jnp.concatenate([packed.full[0:half, :], corner], axis=1),
            jnp.concatenate([corner.T, packed.full[2 * half :, :]], axis=1),
        ],
        axis=0,
    )
    squares = jnp.sum(jnp.sum(gram * gram, axis=0, keepdims=True), axis=1, keepdims=True)
    norm = jnp.sqrt(squares + 1e-06)
    matrix = gram / norm
    m_split = split(matrix)
    square = product(m_split, m_split)
    mixed = product(split(square), split(0.0625 * square - 0.5625 * matrix))
    rows_at = lax.broadcasted_iota(jnp.int32, (width, width), 0)
    cols_at = lax.broadcasted_iota(jnp.int32, (width, width), 1)
    diagonal = jnp.where(rows_at == cols_at, 2.25, 0.0)
    mixed = mixed + (diagonal - 2.4375 * matrix + 1.6875 * square)
    result = product(f_split, split(mixed))
    out[...] = result * (math.sqrt(rows * ring) / jnp.sqrt(norm))

    for copy in net.sent:
        copy.wait_send()
    for part in (first, second, packed):
        part.finish()


def on_device(sizes, ham, cols, start, node_re, node_im, weight_re, weight_im, sweeps):
    rows, width = start.shape
    half = width // 2
    anywhere = pl.BlockSpec(memory_space=pl.ANY)
    scalars = pl.BlockSpec(memory_space=pltpu.SMEM)
    vmem = pltpu.VMEM
    dma = pltpu.SemaphoreType.DMA
    y, zh = max(sizes["y"] - 1, 1), max(sizes["zh"] - 1, 1)
    everyone = sizes["node"] * sizes["x"] * sizes["core"]

    packed = 3 * half
    piece = packed // everyone
    near = sizes["x"] * sizes["core"]
    return pl.pallas_call(
        functools.partial(kernel, sizes),
        out_shape=jax.ShapeDtypeStruct((rows, width), F32),
        in_specs=[anywhere, scalars, anywhere] + [scalars] * 5,
        out_specs=pl.BlockSpec(memory_space=pltpu.VMEM),
        scratch_shapes=[
            vmem(ham.shape, F32),
            vmem((rows, width), F32),
            vmem((2, 2, rows, half), F32),
            vmem((2, rows, half), F32),
            vmem((2, 2, rows, half), F32),
            vmem((rows, 3 * rows), BF16),
            vmem((rows, 3 * rows), BF16),
            vmem((8 * (SWEEPS + 1), 128), F32),
            vmem((8 * (SWEEPS + 1), 128), F32),
            vmem((rows, width), BF16),
            vmem((rows, width), BF16),
            dma((2,)),
            dma((3, 2, 2, 2)),
            dma((3, 2, 2, 2)),
            dma((2,)),
            pltpu.SemaphoreType.REGULAR((3,)),
            vmem((packed, half), F32),
            vmem((near, piece, half), F32),
            vmem((piece, half), F32),
            vmem((y, piece, half), F32),
            vmem((piece, half), F32),
            vmem((zh, piece, half), F32),
            vmem((packed, half), F32),
            dma((2, everyone)),
            dma((2, y)),
            dma((2, zh)),
            dma((2, everyone - 1)),
        ],
        compiler_params=pltpu.CompilerParams(collective_id=0, has_side_effects=True),
    )(ham, cols, start, node_re, node_im, weight_re, weight_im, sweeps)


def build(finer):
    sizes = dict(finer.shape)
    return jax.shard_map(
        functools.partial(on_device, sizes),
        mesh=finer,
        in_specs=(
            P(ROW, None, None, None),
            P(ROW, None),
            P(ROW, None),
            P("node"),
            P("node"),
            P("node"),
            P("node"),
            P("node"),
        ),
        out_specs=P(ROW, None),
        check_vma=False,
    )


def solution(mesh):
    return build(Mesh(mesh.devices.reshape(mesh.shape["node"], 4, 4, 4, 2), AXES))
```

```python
import functools
import itertools
import math

import jax
import jax.numpy as jnp
from jax import lax
from jax.experimental import pallas as pl
from jax.experimental.pallas import tpu as pltpu
from jax.sharding import Mesh
from jax.sharding import PartitionSpec as P

TILE = 128
REACH = 2
SWEEPS = 2
AXES = ("node", "x", "zh", "y", "core")
ROW = AXES[1:]
MESH = pl.DeviceIdType.MESH
F32 = jnp.float32
BF16 = jnp.bfloat16


def split(value):
    high = value.astype(BF16)
    return high, (value - high.astype(F32)).astype(BF16)


def product(left, right, dims=((1,), (0,))):
    def one(a, b):
        return lax.dot_general(a, b, (dims, ((), ())), preferred_element_type=F32)

    return one(left[0], right[0]) + (one(left[0], right[1]) + one(left[1], right[0]))


def pairwise(values):
    count = len(values)
    if count == 1:
        return values[0]
    if count == 2:
        return values[0] + values[1]
    return (values[0] + values[2]) + (values[1] + values[3])


def steps_over(sizes, axes):
    found = [by for by in itertools.product(*(range(sizes[a]) for a in axes)) if any(by)]
    found.sort(key=lambda by: -sum(min(d, sizes[a] - d) for a, d in zip(axes, by) if a != "core"))
    return [dict(zip(axes, by)) for by in found]


class Sum:
    def __init__(self, net, refs):
        self.net = net
        (
            self.part, self.rs_in, self.y_out, self.y_in, self.z_out, self.z_in, self.full,
            self.rs_sem, self.y_sem, self.z_sem, self.ag_sem,
        ) = refs
        self.everyone = steps_over(net.sizes, ("node", "x", "core"))
        self.rows = self.y_out.shape[0]

    def piece(self, at):
        index = 0
        for axis in ("node", "x", "core"):
            index = index * self.net.sizes[axis] + at[axis]
        return pl.ds(pl.multiple_of(index * self.rows, 8), self.rows)

    def partial(self, slot, by):
        peer = self.net.away(**by)
        landing = by["x"] * self.net.sizes["core"] + by["core"]
        return self.net.copy(
            self.part.at[self.piece(peer)],
            self.rs_in.at[landing],
            self.rs_sem.at[0, slot],
            self.rs_sem.at[1, landing],
            peer,
        )

    def scattering(self, by):
        here = jnp.logical_not(self.net.far)
        return here if by["node"] == 0 else here & self.net.edge

    def scatter(self):
        for slot, by in enumerate(self.everyone):

            @pl.when(self.scattering(by))
            def _():
                self.partial(slot, by).start()

    def finish(self):
        for slot, by in enumerate(self.everyone):

            @pl.when(self.scattering(by))
            def _():
                self.partial(slot, by).wait_send()

    def scattered(self):
        ours = self.piece(self.net.me)

        def arrived(landing):
            at = self.rs_in.at[landing]
            self.net.copy(at, at, self.rs_sem.at[0, 0], self.rs_sem.at[1, landing], self.net.away(node=1)).wait_recv()

        @pl.when(self.net.far)
        def _():
            arrived(0)
            self.part[ours, :] = self.rs_in[0]

        value = self.part[ours, :]
        for landing in range(1, self.rs_in.shape[0]):
            arrived(landing)
            value = value + self.rs_in[landing]
        return value

    def order(self, axis):
        size = self.net.sizes[axis]
        return sorted(range(1, size), key=lambda d: -min(d, size - d))

    def share(self, value, axis, source, landing, sem):
        source[...] = value
        self.value = value
        self.landing = landing
        self.copies = [
            self.net.send(source, landing.at[d - 1], sem.at[0, d - 1], sem.at[1, d - 1], self.net.away(**{axis: d}))
            for d in self.order(axis)
        ]

    def shared(self):
        for copy in self.copies:
            copy.wait_recv()
        return pairwise([self.value] + [self.landing[d] for d in range(len(self.copies))])

    def to_y(self):
        self.share(self.scattered(), "y", self.y_out, self.y_in, self.y_sem)

    def to_z(self):
        self.share(self.shared(), "zh", self.z_out, self.z_in, self.z_sem)

    def gather(self):
        value = self.shared()
        ours = self.piece(self.net.me)
        self.full[ours, :] = value
        for slot, by in enumerate(self.everyone):
            self.net.send(
                self.full.at[ours],
                self.full.at[ours],
                self.ag_sem.at[0, slot],
                self.ag_sem.at[1, slot],
                self.net.away(**by),
            )

    def gathered(self):
        for slot, by in enumerate(self.everyone):
            source = self.net.away(**{a: -d for a, d in by.items()})
            theirs = self.full.at[self.piece(source)]
            self.net.copy(
                theirs, theirs, self.ag_sem.at[0, slot], self.ag_sem.at[1, slot], source
            ).wait_recv()


class Net:
    def __init__(self, sizes):
        self.sizes = sizes
        self.me = {a: lax.axis_index(a) for a in AXES}
        self.sent = []
        self.ring = math.prod(sizes[a] for a in ROW)
        me = self.me
        self.position = (
            (me["x"] * sizes["zh"] + me["zh"]) * sizes["y"] + me["y"]
        ) * sizes["core"] + me["core"]
        head = (me["y"] == 0) & (me["core"] == 0)
        tail = (me["y"] == sizes["y"] - 1) & (me["core"] == sizes["core"] - 1)
        self.receives, self.sends = (head, tail), (tail, head)
        self.near = (0, sizes["node"] - 1)
        self.edge = head | tail
        self.filling = (jnp.where(head, 1, 0), jnp.where(head, 0, 1))
        self.far = (head & (me["node"] != self.near[0])) | (tail & (me["node"] != self.near[1]))

    def sending(self, slot):
        return jnp.logical_not(self.sends[slot]) | (self.me["node"] != self.near[slot])

    def target(self, slot):
        node = jnp.where(self.sends[slot], self.near[slot], self.me["node"])
        return {**self.on_ring(1 if slot == 0 else -1), "node": node}

    def relaying(self, slot):
        return self.receives[slot] & (self.me["node"] == self.near[slot])

    def source(self, slot):
        node = jnp.where(self.receives[slot], self.sizes["node"] - 1 - self.near[slot], self.me["node"])
        return {**self.on_ring(-1 if slot == 0 else 1), "node": node}

    def sourced(self, slot):
        return jnp.logical_not(self.receives[slot]) | (self.me["node"] == self.near[slot])

    def away(self, **by):
        return {
            a: lax.rem(self.me[a] + by[a] + self.sizes[a], self.sizes[a]) if by.get(a) else self.me[a]
            for a in AXES
        }

    def on_ring(self, step):
        at = lax.rem(self.position + step + self.ring, self.ring)
        zh, y, core = (self.sizes[a] for a in ("zh", "y", "core"))
        return {
            "node": self.me["node"],
            "x": at // (zh * y * core),
            "zh": lax.rem(at // (y * core), zh),
            "y": lax.rem(at // core, y),
            "core": lax.rem(at, core),
        }

    def copy(self, src, dst, send_sem, recv_sem, peer):
        return pltpu.make_async_remote_copy(
            src_ref=src,
            dst_ref=dst,
            send_sem=send_sem,
            recv_sem=recv_sem,
            device_id=peer,
            device_id_type=MESH,
        )

    def send(self, *what):
        copy = self.copy(*what)
        copy.start()
        self.sent.append(copy)
        return copy


class Halo:
    def __init__(self, net, halo, sem):
        self.net, self.halo, self.sem = net, halo, sem
        self.tile = halo.shape[2] // 2

    def unit(self, slot, c, j):
        return self.halo.at[slot, c, j * self.tile : (j + 1) * self.tile, :]

    def direct(self, src, slot, c, j):
        return self.net.copy(
            src, self.unit(slot, c, j), self.sem.at[0, slot, c, j], self.sem.at[1, slot, c, j], self.net.target(slot)
        )

    def onward(self, slot, c, j):
        at = self.unit(slot, c, j)
        return self.net.copy(
            at, at, self.sem.at[2, slot, c, j], self.sem.at[1, slot, c, j], self.net.away(node=1)
        )

    def send(self, source, c):
        for slot in range(2):

            @pl.when(self.net.sending(slot))
            def _():
                for j in range(2):
                    self.direct(source(c, j), slot, c, j).start()

    def receive(self, c, slot):
        relaying = ((slot == 0) & self.net.relaying(0)) | ((slot == 1) & self.net.relaying(1))
        for j in range(2):
            self.onward(slot, c, j).wait_recv()

            @pl.when(relaying)
            def _():
                self.onward(slot, c, j).start()

    def finish(self):
        for slot in range(2):
            for c, j in itertools.product(range(2), range(2)):

                @pl.when(self.net.sending(slot))
                def _():
                    self.direct(self.unit(slot, c, j), slot, c, j).wait_send()

                @pl.when(self.net.relaying(slot))
                def _():
                    self.onward(slot, c, j).wait_send()


def kernel(
    sizes,
    ham,
    cols_h,
    start,
    node_re_h,
    node_im_h,
    weight_re_h,
    weight_im_h,
    sweeps_h,
    out,
    cols,
    node_re,
    node_im,
    weight_re,
    weight_im,
    sweeps,
    ham_v,
    own,
    halo_v,
    krylov,
    halo1_v,
    band_hi,
    band_lo,
    coef,
    coef_in,
    filt_hi,
    filt_lo,
    local_sem,
    halo_sem,
    halo1_sem,
    coef_sem,
    told,
    *sums,
):
    rows, width = start.shape
    half = width // 2
    net = Net(sizes)
    me, send = net.me, net.send
    position, ring = net.position, net.ring
    twin = net.away(node=1)

    along = [net.away(**{a: d}) for a in ("x", "y", "zh") for d in sorted({1, sizes[a] - 1} - {0})]
    mate = net.away(core=1)
    peers = [mate, twin, *along]
    barrier = pltpu.get_barrier_semaphore()
    greeted = len(peers)
    for slot in range(2):

        @pl.when(net.sourced(slot))
        def _():
            pl.semaphore_signal(barrier, inc=1, device_id=net.source(slot), device_id_type=MESH)

        greeted = greeted + net.sending(slot).astype(jnp.int32)
    for peer in peers:
        pl.semaphore_signal(barrier, inc=1, device_id=peer, device_id_type=MESH)
    ham_copy = pltpu.make_async_copy(ham, ham_v, local_sem.at[0])
    own_copy = pltpu.make_async_copy(start, own, local_sem.at[1])
    few = [
        pltpu.make_async_copy(src, dst, local_sem.at[2 + k])
        for k, (src, dst) in enumerate(
            (
                (cols_h, cols),
                (node_re_h, node_re),
                (node_im_h, node_im),
                (weight_re_h, weight_re),
                (weight_im_h, weight_im),
                (sweeps_h, sweeps),
            )
        )
    ]
    for copy in (*few, ham_copy, own_copy):
        copy.start()
    pl.semaphore_wait(barrier, greeted)

    rounds = (along, [mate, twin], [mate])

    def tell(at):
        for peer in rounds[at]:
            pl.semaphore_signal(told.at[at], inc=1, device_id=peer, device_id_type=MESH)

    def hear(at):
        if rounds[at]:
            pl.semaphore_wait(told.at[at], len(rounds[at]))


    first = Halo(net, halo_v, halo_sem)
    second = Halo(net, halo1_v, halo1_sem)

    def of_start(c, j):
        return start.at[j * TILE : (j + 1) * TILE, c * half : (c + 1) * half]

    def of_krylov(c, j):
        return krylov.at[c, j * TILE : (j + 1) * TILE, :]

    for c in range(2):
        first.send(of_start, c)
    tell(0)

    for copy in few:
        copy.wait()
    listed = [jnp.zeros((8, 128), F32) for _ in range(SWEEPS + 1)]
    for j in range(node_re.shape[0]):
        re, im = jnp.full((8, 128), node_re[j]), jnp.full((8, 128), node_im[j])
        w_re, w_im = jnp.full((8, 128), weight_re[j]), jnp.full((8, 128), weight_im[j])
        count = jnp.full((8, 128), sweeps[j])
        modulus = re * re + im * im
        inverse_re, inverse_im = re / modulus, -im / modulus
        power_re, power_im = inverse_re, inverse_im
        for degree in range(SWEEPS + 1):
            term = w_re * power_re - w_im * power_im
            listed[degree] = listed[degree] + jnp.where(count >= degree, term, 0.0)
            power_re, power_im = (
                power_re * inverse_re - power_im * inverse_im,
                power_re * inverse_im + power_im * inverse_re,
            )
    for degree, value in enumerate(listed):
        coef[8 * degree : 8 * degree + 8, :] = value
    coef_copy = send(coef, coef_in, coef_sem.at[0], coef_sem.at[1], twin)

    ham_copy.wait()
    mine = rows // TILE
    blocks = mine * ring
    for a in range(mine):
        at = position * mine + a
        offset = [
            lax.rem(cols[a, k] - at + REACH + blocks, blocks) for k in range(ham.shape[1])
        ]
        for p in range(3 * mine):
            o = p - a + REACH - mine
            total = jnp.zeros((TILE, TILE), F32)
            if 0 <= o <= 2 * REACH:
                for k in range(ham.shape[1]):
                    fixed = (REACH, 0, 2 * REACH)
                    if k < 3:
                        if fixed[k] == o:
                            total = total + ham_v[a, k]
                    else:
                        total = total + jnp.where(offset[k] == o, 1.0, 0.0) * ham_v[a, k]
            high, low = split(total)
            side, at_p = p // mine, p % mine
            place = (side, slice(a * TILE, (a + 1) * TILE), slice(at_p * TILE, (at_p + 1) * TILE))
            band_hi[place] = high
            band_lo[place] = low

    def band(side):
        return band_hi[side], band_lo[side]

    own_copy.wait()
    parts = []
    for c in range(2):
        parts.append(product(band(1), split(own[:, c * half : (c + 1) * half])))
    for c in range(2):
        total = parts[c]
        for slot in net.filling:
            first.receive(c, slot)
            total = total + product(band(2 * slot), split(halo_v[slot, c]))
        krylov[c] = total
        second.send(of_krylov, c)
        hear(c)
        tell(c + 1)
    hear(2)
    coef_copy.wait_recv()
    scale = [
        (coef[8 * d : 8 * d + 8, :] + coef_in[8 * d : 8 * d + 8, :])[0:1, 0:1]
        for d in range(SWEEPS + 1)
    ]
    parts = [product(band(1), split(krylov[c])) for c in range(2)]
    packed = Sum(net, sums)

    def filter_rows():
        for c in range(2):
            at = slice(c * half, (c + 1) * half)
            total = parts[c]
            for slot in net.filling:
                second.receive(c, slot)
                total = total + product(band(2 * slot), split(halo1_v[slot, c]))
            total = scale[0] * own[:, at] + scale[1] * krylov[c] + scale[2] * total
            filt_hi[:, at], filt_lo[:, at] = split(total)

    @pl.when(jnp.logical_not(net.far))
    def _():
        filter_rows()
        halves = [
            (filt_hi[:, c * half : (c + 1) * half], filt_lo[:, c * half : (c + 1) * half]) for c in range(2)
        ]
        for k, (a, b) in enumerate(((0, 0), (0, 1), (1, 1))):
            packed.part[k * half : (k + 1) * half, :] = product(halves[a], halves[b], ((0,), (0,)))
    packed.scatter()
    packed.to_y()
    packed.to_z()
    packed.gather()
    pl.when(net.far)(filter_rows)
    packed.gathered()
    f_split = (filt_hi[...], filt_lo[...])

    corner = packed.full[half : 2 * half, :]
    gram = jnp.concatenate(
        [
            jnp.concatenate([packed.full[0:half, :], corner], axis=1),
            jnp.concatenate([corner.T, packed.full[2 * half :, :]], axis=1),
        ],
        axis=0,
    )
    squares = jnp.sum(jnp.sum(gram * gram, axis=0, keepdims=True), axis=1, keepdims=True)
    norm = jnp.sqrt(squares + 1e-06)
    scale = math.sqrt(rows * ring) / jnp.sqrt(norm)
    by = 1.0 / norm
    g_split = split(gram)
    square = product(g_split, g_split) * by
    matrix = gram * by
    rows_at = lax.broadcasted_iota(jnp.int32, (width, width), 0)
    cols_at = lax.broadcasted_iota(jnp.int32, (width, width), 1)
    diagonal = jnp.where(rows_at == cols_at, 2.25 * scale, 0.0)
    square = square * by
    low = diagonal - (2.4375 * scale) * matrix + (1.6875 * scale) * square
    mixed = low + product(split(square), split((0.0625 * scale) * square - (0.5625 * scale) * matrix))
    out[...] = product(f_split, split(mixed))

    for copy in net.sent:
        copy.wait_send()
    for part in (first, second, packed):
        part.finish()


def on_device(sizes, ham, cols, start, node_re, node_im, weight_re, weight_im, sweeps):
    rows, width = start.shape
    half = width // 2
    anywhere = pl.BlockSpec(memory_space=pl.ANY)
    smem = pltpu.SMEM
    vmem = pltpu.VMEM
    dma = pltpu.SemaphoreType.DMA
    y, zh = max(sizes["y"] - 1, 1), max(sizes["zh"] - 1, 1)
    everyone = sizes["node"] * sizes["x"] * sizes["core"]

    packed = 3 * half
    piece = packed // everyone
    near = sizes["x"] * sizes["core"]
    ham, cols, start, node_re, node_im, weight_re, weight_im, sweeps = (
        pltpu.with_memory_space_constraint(v, pltpu.HBM)
        for v in (ham, cols, start, node_re, node_im, weight_re, weight_im, sweeps)
    )
    return pl.pallas_call(
        functools.partial(kernel, sizes),
        out_shape=jax.ShapeDtypeStruct((rows, width), F32),
        in_specs=[anywhere] * 8,
        out_specs=pl.BlockSpec(memory_space=pltpu.VMEM),
        scratch_shapes=[
            smem(cols.shape, jnp.int32),
            *[smem(v.shape, F32) for v in (node_re, node_im, weight_re, weight_im)],
            smem(sweeps.shape, jnp.int32),
            vmem(ham.shape, F32),
            vmem((rows, width), F32),
            vmem((2, 2, rows, half), F32),
            vmem((2, rows, half), F32),
            vmem((2, 2, rows, half), F32),
            vmem((3, rows, rows), BF16),
            vmem((3, rows, rows), BF16),
            vmem((8 * (SWEEPS + 1), 128), F32),
            vmem((8 * (SWEEPS + 1), 128), F32),
            vmem((rows, width), BF16),
            vmem((rows, width), BF16),
            dma((8,)),
            dma((3, 2, 2, 2)),
            dma((3, 2, 2, 2)),
            dma((2,)),
            pltpu.SemaphoreType.REGULAR((3,)),
            vmem((packed, half), F32),
            vmem((near, piece, half), F32),
            vmem((piece, half), F32),
            vmem((y, piece, half), F32),
            vmem((piece, half), F32),
            vmem((zh, piece, half), F32),
            vmem((packed, half), F32),
            dma((2, everyone)),
            dma((2, y)),
            dma((2, zh)),
            dma((2, everyone - 1)),
        ],
        compiler_params=pltpu.CompilerParams(collective_id=0, has_side_effects=True, vmem_limit_bytes=40 * 1024 * 1024),
    )(ham, cols, start, node_re, node_im, weight_re, weight_im, sweeps)


def build(finer):
    sizes = dict(finer.shape)
    return jax.shard_map(
        functools.partial(on_device, sizes),
        mesh=finer,
        in_specs=(
            P(ROW, None, None, None),
            P(ROW, None),
            P(ROW, None),
            P("node"),
            P("node"),
            P("node"),
            P("node"),
            P("node"),
        ),
        out_specs=P(ROW, None),
        check_vma=False,
    )


def solution(mesh):
    return build(Mesh(mesh.devices.reshape(mesh.shape["node"], 4, 4, 4, 2), AXES))
```

```python
import functools
import itertools
import math

import jax
import jax.numpy as jnp
from jax import lax
from jax.experimental import pallas as pl
from jax.experimental.pallas import tpu as pltpu
from jax.sharding import Mesh
from jax.sharding import PartitionSpec as P

TILE = 128
REACH = 2
SWEEPS = 2
AXES = ("node", "x", "zh", "y", "core")
ROW = AXES[1:]
MESH = pl.DeviceIdType.MESH
F32 = jnp.float32
BF16 = jnp.bfloat16


def split(value):
    high = value.astype(BF16)
    return high, (value - high.astype(F32)).astype(BF16)


def product(left, right, dims=((1,), (0,))):
    def one(a, b):
        return lax.dot_general(a, b, (dims, ((), ())), preferred_element_type=F32)

    return one(left[0], right[0]) + (one(left[0], right[1]) + one(left[1], right[0]))


def pairwise(values):
    count = len(values)
    if count == 1:
        return values[0]
    if count == 2:
        return values[0] + values[1]
    return (values[0] + values[2]) + (values[1] + values[3])


def steps_over(sizes, axes):
    found = [by for by in itertools.product(*(range(sizes[a]) for a in axes)) if any(by)]
    found.sort(key=lambda by: -sum(min(d, sizes[a] - d) for a, d in zip(axes, by) if a != "core"))
    return [dict(zip(axes, by)) for by in found]


class Sum:
    def __init__(self, net, refs):
        self.net = net
        (
            self.part, self.rs_in, self.y_out, self.y_in, self.z_out, self.z_in, self.full,
            self.rs_sem, self.y_sem, self.z_sem, self.ag_sem,
        ) = refs
        self.everyone = steps_over(net.sizes, ("node", "x", "core"))
        self.rows = self.y_out.shape[0]

    def piece(self, at):
        index = 0
        for axis in ("node", "x", "core"):
            index = index * self.net.sizes[axis] + at[axis]
        return pl.ds(pl.multiple_of(index * self.rows, 8), self.rows)

    def partial(self, slot, by):
        peer = self.net.away(**by)
        landing = by["x"] * self.net.sizes["core"] + by["core"]
        return self.net.copy(
            self.part.at[self.piece(peer)],
            self.rs_in.at[landing],
            self.rs_sem.at[0, slot],
            self.rs_sem.at[1, landing],
            peer,
        )

    def scattering(self, by):
        here = jnp.logical_not(self.net.far)
        return here if by["node"] == 0 else here & self.net.edge

    def scatter(self):
        for slot, by in enumerate(self.everyone):

            @pl.when(self.scattering(by))
            def _():
                self.partial(slot, by).start()

    def finish(self):
        for slot, by in enumerate(self.everyone):

            @pl.when(self.scattering(by))
            def _():
                self.partial(slot, by).wait_send()

    def scattered(self):
        ours = self.piece(self.net.me)

        def arrived(landing):
            at = self.rs_in.at[landing]
            self.net.copy(at, at, self.rs_sem.at[0, 0], self.rs_sem.at[1, landing], self.net.away(node=1)).wait_recv()

        @pl.when(self.net.far)
        def _():
            arrived(0)
            self.part[ours, :] = self.rs_in[0]

        value = self.part[ours, :]
        for landing in range(1, self.rs_in.shape[0]):
            arrived(landing)
            value = value + self.rs_in[landing]
        return value

    def order(self, axis):
        size = self.net.sizes[axis]
        return sorted(range(1, size), key=lambda d: -min(d, size - d))

    def share(self, value, axis, source, landing, sem):
        source[...] = value
        self.value = value
        self.landing = landing
        self.copies = [
            self.net.send(source, landing.at[d - 1], sem.at[0, d - 1], sem.at[1, d - 1], self.net.away(**{axis: d}))
            for d in self.order(axis)
        ]

    def shared(self):
        for copy in self.copies:
            copy.wait_recv()
        return pairwise([self.value] + [self.landing[d] for d in range(len(self.copies))])

    def to_z(self):
        self.share(self.scattered(), "zh", self.z_out, self.z_in, self.z_sem)

    def to_y(self):
        self.share(self.shared(), "y", self.y_out, self.y_in, self.y_sem)

    def gather(self):
        value = self.shared()
        ours = self.piece(self.net.me)
        self.full[ours, :] = value
        for slot, by in enumerate(self.everyone):
            self.net.send(
                self.full.at[ours],
                self.full.at[ours],
                self.ag_sem.at[0, slot],
                self.ag_sem.at[1, slot],
                self.net.away(**by),
            )

    def gathered(self):
        for slot, by in enumerate(self.everyone):
            source = self.net.away(**{a: -d for a, d in by.items()})
            theirs = self.full.at[self.piece(source)]
            self.net.copy(
                theirs, theirs, self.ag_sem.at[0, slot], self.ag_sem.at[1, slot], source
            ).wait_recv()


class Net:
    def __init__(self, sizes):
        self.sizes = sizes
        self.me = {a: lax.axis_index(a) for a in AXES}
        self.sent = []
        self.ring = math.prod(sizes[a] for a in ROW)
        me = self.me
        self.position = (
            (me["x"] * sizes["zh"] + me["zh"]) * sizes["y"] + me["y"]
        ) * sizes["core"] + me["core"]
        head = (me["y"] == 0) & (me["core"] == 0)
        tail = (me["y"] == sizes["y"] - 1) & (me["core"] == sizes["core"] - 1)
        self.receives, self.sends = (head, tail), (tail, head)
        self.near = (0, sizes["node"] - 1)
        self.edge = head | tail
        self.filling = (jnp.where(head, 1, 0), jnp.where(head, 0, 1))
        self.far = (head & (me["node"] != self.near[0])) | (tail & (me["node"] != self.near[1]))

    def sending(self, slot):
        return jnp.logical_not(self.sends[slot]) | (self.me["node"] != self.near[slot])

    def target(self, slot):
        node = jnp.where(self.sends[slot], self.near[slot], self.me["node"])
        return {**self.on_ring(1 if slot == 0 else -1), "node": node}

    def relaying(self, slot):
        return self.receives[slot] & (self.me["node"] == self.near[slot])

    def source(self, slot):
        node = jnp.where(self.receives[slot], self.sizes["node"] - 1 - self.near[slot], self.me["node"])
        return {**self.on_ring(-1 if slot == 0 else 1), "node": node}

    def sourced(self, slot):
        return jnp.logical_not(self.receives[slot]) | (self.me["node"] == self.near[slot])

    def away(self, **by):
        return {
            a: lax.rem(self.me[a] + by[a] + self.sizes[a], self.sizes[a]) if by.get(a) else self.me[a]
            for a in AXES
        }

    def on_ring(self, step):
        at = lax.rem(self.position + step + self.ring, self.ring)
        zh, y, core = (self.sizes[a] for a in ("zh", "y", "core"))
        return {
            "node": self.me["node"],
            "x": at // (zh * y * core),
            "zh": lax.rem(at // (y * core), zh),
            "y": lax.rem(at // core, y),
            "core": lax.rem(at, core),
        }

    def copy(self, src, dst, send_sem, recv_sem, peer):
        return pltpu.make_async_remote_copy(
            src_ref=src,
            dst_ref=dst,
            send_sem=send_sem,
            recv_sem=recv_sem,
            device_id=peer,
            device_id_type=MESH,
        )

    def send(self, *what):
        copy = self.copy(*what)
        copy.start()
        self.sent.append(copy)
        return copy


class Halo:
    def __init__(self, net, halo, sem, later=False):
        self.net, self.halo, self.sem, self.later = net, halo, sem, later
        self.tile = halo.shape[2] // 2

    def unit(self, slot, c, j):
        return self.halo.at[slot, c, j * self.tile : (j + 1) * self.tile, :]

    def direct(self, src, slot, c, j):
        return self.net.copy(
            src, self.unit(slot, c, j), self.sem.at[0, slot, c, j], self.sem.at[1, slot, c, j], self.net.target(slot)
        )

    def onward(self, slot, c, j):
        at = self.unit(slot, c, j)
        return self.net.copy(
            at, at, self.sem.at[2, slot, c, j], self.sem.at[1, slot, c, j], self.net.away(node=1)
        )

    def send(self, source, c):
        for slot in range(2):

            @pl.when(self.net.sending(slot))
            def _():
                for j in range(2):
                    self.direct(source(c, j), slot, c, j).start()

    def receive(self, c, slot):
        relaying = ((slot == 0) & self.net.relaying(0)) | ((slot == 1) & self.net.relaying(1))
        for j in range(2):
            self.onward(slot, c, j).wait_recv()

            if not self.later:

                @pl.when(relaying)
                def _():
                    self.onward(slot, c, j).start()

    def relay(self):
        for slot, c, j in itertools.product(range(2), range(2), range(2)):

            @pl.when(self.net.relaying(slot))
            def _():
                self.onward(slot, c, j).start()

    def finish(self):
        for slot in range(2):
            for c, j in itertools.product(range(2), range(2)):

                @pl.when(self.net.sending(slot))
                def _():
                    self.direct(self.unit(slot, c, j), slot, c, j).wait_send()

                @pl.when(self.net.relaying(slot))
                def _():
                    self.onward(slot, c, j).wait_send()


def kernel(
    sizes,
    ham,
    cols_h,
    start,
    node_re_h,
    node_im_h,
    weight_re_h,
    weight_im_h,
    sweeps_h,
    out,
    cols,
    node_re,
    node_im,
    weight_re,
    weight_im,
    sweeps,
    ham_v,
    own,
    halo_v,
    krylov,
    halo1_v,
    band_hi,
    band_lo,
    coef,
    coef_in,
    filt_hi,
    filt_lo,
    local_sem,
    halo_sem,
    halo1_sem,
    coef_sem,
    told,
    *sums,
):
    rows, width = start.shape
    half = width // 2
    net = Net(sizes)
    me, send = net.me, net.send
    position, ring = net.position, net.ring
    twin = net.away(node=1)

    along = [net.away(**{a: d}) for a in ("x", "y", "zh") for d in sorted({1, sizes[a] - 1} - {0})]
    mate = net.away(core=1)
    peers = [mate, twin, *along]
    barrier = pltpu.get_barrier_semaphore()
    greeted = len(peers)
    for slot in range(2):

        @pl.when(net.sourced(slot))
        def _():
            pl.semaphore_signal(barrier, inc=1, device_id=net.source(slot), device_id_type=MESH)

        greeted = greeted + net.sending(slot).astype(jnp.int32)
    for peer in peers:
        pl.semaphore_signal(barrier, inc=1, device_id=peer, device_id_type=MESH)
    ham_copy = pltpu.make_async_copy(ham, ham_v, local_sem.at[0])
    own_copy = pltpu.make_async_copy(start, own, local_sem.at[1])
    few = [
        pltpu.make_async_copy(src, dst, local_sem.at[2 + k])
        for k, (src, dst) in enumerate(
            (
                (cols_h, cols),
                (node_re_h, node_re),
                (node_im_h, node_im),
                (weight_re_h, weight_re),
                (weight_im_h, weight_im),
                (sweeps_h, sweeps),
            )
        )
    ]
    for copy in (*few, ham_copy, own_copy):
        copy.start()
    pl.semaphore_wait(barrier, greeted)

    rounds = (along, [mate, twin], [mate])

    def tell(at):
        for peer in rounds[at]:
            pl.semaphore_signal(told.at[at], inc=1, device_id=peer, device_id_type=MESH)

    def hear(at):
        if rounds[at]:
            pl.semaphore_wait(told.at[at], len(rounds[at]))


    first = Halo(net, halo_v, halo_sem)
    second = Halo(net, halo1_v, halo1_sem, later=True)

    def of_start(c, j):
        return start.at[j * TILE : (j + 1) * TILE, c * half : (c + 1) * half]

    def of_krylov(c, j):
        return krylov.at[c, j * TILE : (j + 1) * TILE, :]

    for c in range(2):
        first.send(of_start, c)
    tell(0)

    for copy in few:
        copy.wait()
    listed = [jnp.zeros((8, 128), F32) for _ in range(SWEEPS + 1)]
    for j in range(node_re.shape[0]):
        re, im = jnp.full((8, 128), node_re[j]), jnp.full((8, 128), node_im[j])
        w_re, w_im = jnp.full((8, 128), weight_re[j]), jnp.full((8, 128), weight_im[j])
        count = jnp.full((8, 128), sweeps[j])
        modulus = re * re + im * im
        inverse_re, inverse_im = re / modulus, -im / modulus
        power_re, power_im = inverse_re, inverse_im
        for degree in range(SWEEPS + 1):
            term = w_re * power_re - w_im * power_im
            listed[degree] = listed[degree] + jnp.where(count >= degree, term, 0.0)
            power_re, power_im = (
                power_re * inverse_re - power_im * inverse_im,
                power_re * inverse_im + power_im * inverse_re,
            )
    for degree, value in enumerate(listed):
        coef[8 * degree : 8 * degree + 8, :] = value
    coef_copy = send(coef, coef_in, coef_sem.at[0], coef_sem.at[1], twin)

    ham_copy.wait()
    mine = rows // TILE
    blocks = mine * ring
    for a in range(mine):
        at = position * mine + a
        offset = [
            lax.rem(cols[a, k] - at + REACH + blocks, blocks) for k in range(ham.shape[1])
        ]
        for p in range(3 * mine):
            o = p - a + REACH - mine
            total = jnp.zeros((TILE, TILE), F32)
            if 0 <= o <= 2 * REACH:
                for k in range(ham.shape[1]):
                    fixed = (REACH, 0, 2 * REACH)
                    if k < 3:
                        if fixed[k] == o:
                            total = total + ham_v[a, k]
                    else:
                        total = total + jnp.where(offset[k] == o, 1.0, 0.0) * ham_v[a, k]
            high, low = split(total)
            side, at_p = p // mine, p % mine
            place = (side, slice(a * TILE, (a + 1) * TILE), slice(at_p * TILE, (at_p + 1) * TILE))
            band_hi[place] = high
            band_lo[place] = low

    def band(side):
        return band_hi[side], band_lo[side]

    own_copy.wait()
    parts = []
    for c in range(2):
        parts.append(product(band(1), split(own[:, c * half : (c + 1) * half])))
    for c in range(2):
        total = parts[c]
        for slot in net.filling:
            first.receive(c, slot)
            total = total + product(band(2 * slot), split(halo_v[slot, c]))
        krylov[c] = total
        second.send(of_krylov, c)
        hear(c)
        tell(c + 1)
    hear(2)
    coef_copy.wait_recv()
    scale = [
        (coef[8 * d : 8 * d + 8, :] + coef_in[8 * d : 8 * d + 8, :])[0:1, 0:1]
        for d in range(SWEEPS + 1)
    ]
    parts = [product(band(1), split(krylov[c])) for c in range(2)]
    packed = Sum(net, sums)

    def filter_rows():
        for c in range(2):
            at = slice(c * half, (c + 1) * half)
            total = parts[c]
            for slot in net.filling:
                second.receive(c, slot)
                total = total + product(band(2 * slot), split(halo1_v[slot, c]))
            total = scale[0] * own[:, at] + scale[1] * krylov[c] + scale[2] * total
            filt_hi[:, at], filt_lo[:, at] = split(total)

    @pl.when(jnp.logical_not(net.far))
    def _():
        filter_rows()
        halves = [
            (filt_hi[:, c * half : (c + 1) * half], filt_lo[:, c * half : (c + 1) * half]) for c in range(2)
        ]
        for k, (a, b) in enumerate(((0, 0), (0, 1), (1, 1))):
            packed.part[k * half : (k + 1) * half, :] = product(halves[a], halves[b], ((0,), (0,)))
    packed.scatter()
    second.relay()
    packed.to_z()
    packed.to_y()
    packed.gather()
    pl.when(net.far)(filter_rows)
    packed.gathered()
    f_split = (filt_hi[...], filt_lo[...])

    corner = packed.full[half : 2 * half, :]
    gram = jnp.concatenate(
        [
            jnp.concatenate([packed.full[0:half, :], corner], axis=1),
            jnp.concatenate([corner.T, packed.full[2 * half :, :]], axis=1),
        ],
        axis=0,
    )
    squares = jnp.sum(jnp.sum(gram * gram, axis=0, keepdims=True), axis=1, keepdims=True)
    norm = jnp.sqrt(squares + 1e-06)
    scale = math.sqrt(rows * ring) / jnp.sqrt(norm)
    by = 1.0 / norm
    g_split = split(gram)
    square = product(g_split, g_split) * by
    matrix = gram * by
    rows_at = lax.broadcasted_iota(jnp.int32, (width, width), 0)
    cols_at = lax.broadcasted_iota(jnp.int32, (width, width), 1)
    diagonal = jnp.where(rows_at == cols_at, 2.25 * scale, 0.0)
    square = square * by
    low = diagonal - (2.4375 * scale) * matrix + (1.6875 * scale) * square
    mixed = low + product(split(square), split((0.0625 * scale) * square - (0.5625 * scale) * matrix))
    out[...] = product(f_split, split(mixed))

    for copy in net.sent:
        copy.wait_send()
    for part in (first, second, packed):
        part.finish()


def on_device(sizes, ham, cols, start, node_re, node_im, weight_re, weight_im, sweeps):
    rows, width = start.shape
    half = width // 2
    anywhere = pl.BlockSpec(memory_space=pl.ANY)
    smem = pltpu.SMEM
    vmem = pltpu.VMEM
    dma = pltpu.SemaphoreType.DMA
    y, zh = max(sizes["y"] - 1, 1), max(sizes["zh"] - 1, 1)
    everyone = sizes["node"] * sizes["x"] * sizes["core"]

    packed = 3 * half
    piece = packed // everyone
    near = sizes["x"] * sizes["core"]
    ham, cols, start, node_re, node_im, weight_re, weight_im, sweeps = (
        pltpu.with_memory_space_constraint(v, pltpu.HBM)
        for v in (ham, cols, start, node_re, node_im, weight_re, weight_im, sweeps)
    )
    return pl.pallas_call(
        functools.partial(kernel, sizes),
        out_shape=jax.ShapeDtypeStruct((rows, width), F32),
        in_specs=[anywhere] * 8,
        out_specs=pl.BlockSpec(memory_space=pltpu.VMEM),
        scratch_shapes=[
            smem(cols.shape, jnp.int32),
            *[smem(v.shape, F32) for v in (node_re, node_im, weight_re, weight_im)],
            smem(sweeps.shape, jnp.int32),
            vmem(ham.shape, F32),
            vmem((rows, width), F32),
            vmem((2, 2, rows, half), F32),
            vmem((2, rows, half), F32),
            vmem((2, 2, rows, half), F32),
            vmem((3, rows, rows), BF16),
            vmem((3, rows, rows), BF16),
            vmem((8 * (SWEEPS + 1), 128), F32),
            vmem((8 * (SWEEPS + 1), 128), F32),
            vmem((rows, width), BF16),
            vmem((rows, width), BF16),
            dma((8,)),
            dma((3, 2, 2, 2)),
            dma((3, 2, 2, 2)),
            dma((2,)),
            pltpu.SemaphoreType.REGULAR((3,)),
            vmem((packed, half), F32),
            vmem((near, piece, half), F32),
            vmem((piece, half), F32),
            vmem((y, piece, half), F32),
            vmem((piece, half), F32),
            vmem((zh, piece, half), F32),
            vmem((packed, half), F32),
            dma((2, everyone)),
            dma((2, y)),
            dma((2, zh)),
            dma((2, everyone - 1)),
        ],
        compiler_params=pltpu.CompilerParams(collective_id=0, has_side_effects=True, vmem_limit_bytes=40 * 1024 * 1024),
    )(ham, cols, start, node_re, node_im, weight_re, weight_im, sweeps)


def build(finer):
    sizes = dict(finer.shape)
    return jax.shard_map(
        functools.partial(on_device, sizes),
        mesh=finer,
        in_specs=(
            P(ROW, None, None, None),
            P(ROW, None),
            P(ROW, None),
            P("node"),
            P("node"),
            P("node"),
            P("node"),
            P("node"),
        ),
        out_specs=P(ROW, None),
        check_vma=False,
    )


def solution(mesh):
    return build(Mesh(mesh.devices.reshape(mesh.shape["node"], 4, 4, 4, 2), AXES))
```

```python
import functools
import itertools
import math

import jax
import jax.numpy as jnp
from jax import lax
from jax.experimental import pallas as pl
from jax.experimental.pallas import tpu as pltpu
from jax.sharding import Mesh
from jax.sharding import PartitionSpec as P

TILE = 128
REACH = 2
SWEEPS = 2
AXES = ("node", "x", "zh", "y", "core")
ROW = AXES[1:]
MESH = pl.DeviceIdType.MESH
F32 = jnp.float32
BF16 = jnp.bfloat16


def split(value):
    high = value.astype(BF16)
    return high, (value - high.astype(F32)).astype(BF16)


def product(left, right, dims=((1,), (0,))):
    def one(a, b):
        return lax.dot_general(a, b, (dims, ((), ())), preferred_element_type=F32)

    return one(left[0], right[0]) + (one(left[0], right[1]) + one(left[1], right[0]))


def pairwise(values):
    count = len(values)
    if count == 1:
        return values[0]
    if count == 2:
        return values[0] + values[1]
    return (values[0] + values[2]) + (values[1] + values[3])


def steps_over(sizes, axes):
    found = [by for by in itertools.product(*(range(sizes[a]) for a in axes)) if any(by)]
    found.sort(key=lambda by: -sum(min(d, sizes[a] - d) for a, d in zip(axes, by) if a != "core"))
    return [dict(zip(axes, by)) for by in found]


class Sum:
    def __init__(self, net, refs):
        self.net = net
        (
            self.part, self.rs_in, self.y_out, self.y_in, self.z_out, self.z_in, self.full,
            self.rs_sem, self.y_sem, self.z_sem, self.ag_sem,
        ) = refs
        self.everyone = steps_over(net.sizes, ("node", "x", "core"))
        self.rows = self.y_out.shape[0]

    def piece(self, at):
        index = 0
        for axis in ("node", "x", "core"):
            index = index * self.net.sizes[axis] + at[axis]
        return pl.ds(pl.multiple_of(index * self.rows, 8), self.rows)

    def partial(self, slot, by):
        peer = self.net.away(**by)
        landing = by["x"] * self.net.sizes["core"] + by["core"]
        return self.net.copy(
            self.part.at[self.piece(peer)],
            self.rs_in.at[landing],
            self.rs_sem.at[0, slot],
            self.rs_sem.at[1, landing],
            peer,
        )

    def scattering(self, by):
        here = jnp.logical_not(self.net.far)
        return here if by["node"] == 0 else here & self.net.edge

    def scatter(self):
        for slot, by in enumerate(self.everyone):

            @pl.when(self.scattering(by))
            def _():
                self.partial(slot, by).start()

    def finish(self):
        for slot, by in enumerate(self.everyone):

            @pl.when(self.scattering(by))
            def _():
                self.partial(slot, by).wait_send()

    def scattered(self):
        ours = self.piece(self.net.me)

        def arrived(landing):
            at = self.rs_in.at[landing]
            self.net.copy(at, at, self.rs_sem.at[0, 0], self.rs_sem.at[1, landing], self.net.away(node=1)).wait_recv()

        @pl.when(self.net.far)
        def _():
            arrived(0)
            self.part[ours, :] = self.rs_in[0]

        value = self.part[ours, :]
        for landing in range(1, self.rs_in.shape[0]):
            arrived(landing)
            value = value + self.rs_in[landing]
        return value

    def order(self, axis):
        size = self.net.sizes[axis]
        return sorted(range(1, size), key=lambda d: -min(d, size - d))

    def share(self, value, axis, source, landing, sem):
        source[...] = value
        self.value = value
        self.landing = landing
        self.copies = [
            self.net.send(source, landing.at[d - 1], sem.at[0, d - 1], sem.at[1, d - 1], self.net.away(**{axis: d}))
            for d in self.order(axis)
        ]

    def shared(self):
        for copy in self.copies:
            copy.wait_recv()
        return pairwise([self.value] + [self.landing[d] for d in range(len(self.copies))])

    def to_z(self):
        self.share(self.scattered(), "zh", self.z_out, self.z_in, self.z_sem)

    def to_y(self):
        self.share(self.shared(), "y", self.y_out, self.y_in, self.y_sem)

    def gather(self):
        value = self.shared()
        ours = self.piece(self.net.me)
        self.full[ours, :] = value
        for slot, by in enumerate(self.everyone):
            self.net.send(
                self.full.at[ours],
                self.full.at[ours],
                self.ag_sem.at[0, slot],
                self.ag_sem.at[1, slot],
                self.net.away(**by),
            )

    def gathered(self):
        for slot, by in enumerate(self.everyone):
            source = self.net.away(**{a: -d for a, d in by.items()})
            theirs = self.full.at[self.piece(source)]
            self.net.copy(
                theirs, theirs, self.ag_sem.at[0, slot], self.ag_sem.at[1, slot], source
            ).wait_recv()


class Net:
    def __init__(self, sizes):
        self.sizes = sizes
        self.me = {a: lax.axis_index(a) for a in AXES}
        self.sent = []
        self.ring = math.prod(sizes[a] for a in ROW)
        me = self.me
        self.position = (
            (me["x"] * sizes["zh"] + me["zh"]) * sizes["y"] + me["y"]
        ) * sizes["core"] + me["core"]
        head = (me["y"] == 0) & (me["core"] == 0)
        tail = (me["y"] == sizes["y"] - 1) & (me["core"] == sizes["core"] - 1)
        self.receives, self.sends = (head, tail), (tail, head)
        self.near = (0, sizes["node"] - 1)
        self.edge = head | tail
        self.filling = (jnp.where(head, 1, 0), jnp.where(head, 0, 1))
        self.far = (head & (me["node"] != self.near[0])) | (tail & (me["node"] != self.near[1]))

    def sending(self, slot):
        return jnp.logical_not(self.sends[slot]) | (self.me["node"] != self.near[slot])

    def target(self, slot):
        node = jnp.where(self.sends[slot], self.near[slot], self.me["node"])
        return {**self.on_ring(1 if slot == 0 else -1), "node": node}

    def relaying(self, slot):
        return self.receives[slot] & (self.me["node"] == self.near[slot])

    def source(self, slot):
        node = jnp.where(self.receives[slot], self.sizes["node"] - 1 - self.near[slot], self.me["node"])
        return {**self.on_ring(-1 if slot == 0 else 1), "node": node}

    def sourced(self, slot):
        return jnp.logical_not(self.receives[slot]) | (self.me["node"] == self.near[slot])

    def away(self, **by):
        return {
            a: lax.rem(self.me[a] + by[a] + self.sizes[a], self.sizes[a]) if by.get(a) else self.me[a]
            for a in AXES
        }

    def on_ring(self, step):
        at = lax.rem(self.position + step + self.ring, self.ring)
        zh, y, core = (self.sizes[a] for a in ("zh", "y", "core"))
        return {
            "node": self.me["node"],
            "x": at // (zh * y * core),
            "zh": lax.rem(at // (y * core), zh),
            "y": lax.rem(at // core, y),
            "core": lax.rem(at, core),
        }

    def copy(self, src, dst, send_sem, recv_sem, peer):
        return pltpu.make_async_remote_copy(
            src_ref=src,
            dst_ref=dst,
            send_sem=send_sem,
            recv_sem=recv_sem,
            device_id=peer,
            device_id_type=MESH,
        )

    def send(self, *what):
        copy = self.copy(*what)
        copy.start()
        self.sent.append(copy)
        return copy


class Halo:
    def __init__(self, net, halo, sem, later=False):
        self.net, self.halo, self.sem, self.later = net, halo, sem, later
        self.tile = halo.shape[2] // 2

    def unit(self, slot, c, j):
        return self.halo.at[slot, c, j * self.tile : (j + 1) * self.tile, :]

    def direct(self, src, slot, c, j):
        return self.net.copy(
            src, self.unit(slot, c, j), self.sem.at[0, slot, c, j], self.sem.at[1, slot, c, j], self.net.target(slot)
        )

    def onward(self, slot, c, j):
        at = self.unit(slot, c, j)
        return self.net.copy(
            at, at, self.sem.at[2, slot, c, j], self.sem.at[1, slot, c, j], self.net.away(node=1)
        )

    def send(self, source, c):
        for slot in range(2):

            @pl.when(self.net.sending(slot))
            def _():
                for j in range(2):
                    self.direct(source(c, j), slot, c, j).start()

    def receive(self, c, slot):
        relaying = ((slot == 0) & self.net.relaying(0)) | ((slot == 1) & self.net.relaying(1))
        for j in range(2):
            self.onward(slot, c, j).wait_recv()

            if not self.later:

                @pl.when(relaying)
                def _():
                    self.onward(slot, c, j).start()

    def relay(self):
        for slot, c, j in itertools.product(range(2), range(2), range(2)):

            @pl.when(self.net.relaying(slot))
            def _():
                self.onward(slot, c, j).start()

    def finish(self):
        for slot in range(2):
            for c, j in itertools.product(range(2), range(2)):

                @pl.when(self.net.sending(slot))
                def _():
                    self.direct(self.unit(slot, c, j), slot, c, j).wait_send()

                @pl.when(self.net.relaying(slot))
                def _():
                    self.onward(slot, c, j).wait_send()


def kernel(
    sizes,
    ham,
    cols_h,
    start,
    node_re_h,
    node_im_h,
    weight_re_h,
    weight_im_h,
    sweeps_h,
    out,
    cols,
    node_re,
    node_im,
    weight_re,
    weight_im,
    sweeps,
    ham_v,
    own,
    halo_v,
    krylov,
    halo1_v,
    band_hi,
    band_lo,
    coef,
    coef_in,
    filt_hi,
    filt_lo,
    local_sem,
    halo_sem,
    halo1_sem,
    coef_sem,
    told,
    *sums,
):
    rows, width = start.shape
    half = width // 2
    net = Net(sizes)
    me, send = net.me, net.send
    position, ring = net.position, net.ring
    twin = net.away(node=1)

    along = [net.away(**{a: d}) for a in ("x", "y", "zh") for d in sorted({1, sizes[a] - 1} - {0})]
    mate = net.away(core=1)
    peers = [mate, twin, *along]
    barrier = pltpu.get_barrier_semaphore()
    greeted = len(peers)
    for slot in range(2):

        @pl.when(net.sourced(slot))
        def _():
            pl.semaphore_signal(barrier, inc=1, device_id=net.source(slot), device_id_type=MESH)

        greeted = greeted + net.sending(slot).astype(jnp.int32)
    for peer in peers:
        pl.semaphore_signal(barrier, inc=1, device_id=peer, device_id_type=MESH)
    ham_copy = pltpu.make_async_copy(ham, ham_v, local_sem.at[0])
    own_copy = pltpu.make_async_copy(start, own, local_sem.at[1])
    few = [
        pltpu.make_async_copy(src, dst, local_sem.at[2 + k])
        for k, (src, dst) in enumerate(
            (
                (cols_h, cols),
                (node_re_h, node_re),
                (node_im_h, node_im),
                (weight_re_h, weight_re),
                (weight_im_h, weight_im),
                (sweeps_h, sweeps),
            )
        )
    ]
    for copy in (*few, ham_copy, own_copy):
        copy.start()
    pl.semaphore_wait(barrier, greeted)

    rounds = (along, [mate, twin], [mate])

    def tell(at):
        for peer in rounds[at]:
            pl.semaphore_signal(told.at[at], inc=1, device_id=peer, device_id_type=MESH)

    def hear(at):
        if rounds[at]:
            pl.semaphore_wait(told.at[at], len(rounds[at]))


    first = Halo(net, halo_v, halo_sem)
    second = Halo(net, halo1_v, halo1_sem, later=True)

    def of_start(c, j):
        return start.at[j * TILE : (j + 1) * TILE, c * half : (c + 1) * half]

    def of_krylov(c, j):
        return krylov.at[c, j * TILE : (j + 1) * TILE, :]

    for c in range(2):
        first.send(of_start, c)
    tell(0)

    for copy in few:
        copy.wait()
    listed = [jnp.zeros((8, 128), F32) for _ in range(SWEEPS + 1)]
    for j in range(node_re.shape[0]):
        re, im = jnp.full((8, 128), node_re[j]), jnp.full((8, 128), node_im[j])
        w_re, w_im = jnp.full((8, 128), weight_re[j]), jnp.full((8, 128), weight_im[j])
        count = jnp.full((8, 128), sweeps[j])
        modulus = re * re + im * im
        inverse_re, inverse_im = re / modulus, -im / modulus
        power_re, power_im = inverse_re, inverse_im
        for degree in range(SWEEPS + 1):
            term = w_re * power_re - w_im * power_im
            listed[degree] = listed[degree] + jnp.where(count >= degree, term, 0.0)
            power_re, power_im = (
                power_re * inverse_re - power_im * inverse_im,
                power_re * inverse_im + power_im * inverse_re,
            )
    for degree, value in enumerate(listed):
        coef[8 * degree : 8 * degree + 8, :] = value
    coef_copy = send(coef, coef_in, coef_sem.at[0], coef_sem.at[1], twin)

    ham_copy.wait()
    mine = rows // TILE
    blocks = mine * ring
    for a in range(mine):
        at = position * mine + a
        offset = [
            lax.rem(cols[a, k] - at + REACH + blocks, blocks) for k in range(ham.shape[1])
        ]
        for p in range(3 * mine):
            o = p - a + REACH - mine
            total = jnp.zeros((TILE, TILE), F32)
            if 0 <= o <= 2 * REACH:
                for k in range(ham.shape[1]):
                    fixed = (REACH, 0, 2 * REACH)
                    if k < 3:
                        if fixed[k] == o:
                            total = total + ham_v[a, k]
                    else:
                        total = total + jnp.where(offset[k] == o, 1.0, 0.0) * ham_v[a, k]
            high, low = split(total)
            side, at_p = p // mine, p % mine
            place = (side, slice(a * TILE, (a + 1) * TILE), slice(at_p * TILE, (at_p + 1) * TILE))
            band_hi[place] = high
            band_lo[place] = low

    def band(side):
        return band_hi[side], band_lo[side]

    own_copy.wait()
    parts = []
    for c in range(2):
        parts.append(product(band(1), split(own[:, c * half : (c + 1) * half])))
    for c in range(2):
        total = parts[c]
        for slot in net.filling:
            first.receive(c, slot)
            total = total + product(band(2 * slot), split(halo_v[slot, c]))
        krylov[c] = total
        second.send(of_krylov, c)
        hear(c)
        tell(c + 1)
    hear(2)
    coef_copy.wait_recv()
    scale = [
        (coef[8 * d : 8 * d + 8, :] + coef_in[8 * d : 8 * d + 8, :])[0:1, 0:1]
        for d in range(SWEEPS + 1)
    ]
    parts = [product(band(1), split(krylov[c])) for c in range(2)]
    packed = Sum(net, sums)

    def filter_rows():
        for c in range(2):
            at = slice(c * half, (c + 1) * half)
            total = parts[c]
            for slot in net.filling:
                second.receive(c, slot)
                total = total + product(band(2 * slot), split(halo1_v[slot, c]))
            total = scale[0] * own[:, at] + scale[1] * krylov[c] + scale[2] * total
            filt_hi[:, at], filt_lo[:, at] = split(total)

    @pl.when(jnp.logical_not(net.far))
    def _():
        filter_rows()
        halves = [
            (filt_hi[:, c * half : (c + 1) * half], filt_lo[:, c * half : (c + 1) * half]) for c in range(2)
        ]
        for k, (a, b) in enumerate(((0, 0), (0, 1), (1, 1))):
            packed.part[k * half : (k + 1) * half, :] = product(halves[a], halves[b], ((0,), (0,)))
    packed.scatter()
    second.relay()
    packed.to_z()
    packed.to_y()
    packed.gather()
    pl.when(net.far)(filter_rows)
    packed.gathered()
    f_split = (filt_hi[...], filt_lo[...])

    corner = packed.full[half : 2 * half, :]
    gram = jnp.concatenate(
        [
            jnp.concatenate([packed.full[0:half, :], corner], axis=1),
            jnp.concatenate([corner.T, packed.full[2 * half :, :]], axis=1),
        ],
        axis=0,
    )
    squares = jnp.sum(jnp.sum(gram * gram, axis=0, keepdims=True), axis=1, keepdims=True)
    norm = jnp.sqrt(squares + 1e-06)
    scale = math.sqrt(rows * ring) / jnp.sqrt(norm)
    by = 1.0 / norm
    g_split = split(gram)
    square = product(g_split, g_split) * (by * by)
    rows_at = lax.broadcasted_iota(jnp.int32, (width, width), 0)
    cols_at = lax.broadcasted_iota(jnp.int32, (width, width), 1)
    diagonal = jnp.where(rows_at == cols_at, 2.25 * scale, 0.0)
    low = diagonal - (2.4375 * scale * by) * gram + (1.6875 * scale) * square
    rest = (0.0625 * scale) * square - (0.5625 * scale * by) * gram
    mixed = low + product(split(square), split(rest))
    out[...] = product(f_split, split(mixed))

    for copy in net.sent:
        copy.wait_send()
    for part in (first, second, packed):
        part.finish()


def on_device(sizes, ham, cols, start, node_re, node_im, weight_re, weight_im, sweeps):
    rows, width = start.shape
    half = width // 2
    anywhere = pl.BlockSpec(memory_space=pl.ANY)
    smem = pltpu.SMEM
    vmem = pltpu.VMEM
    dma = pltpu.SemaphoreType.DMA
    y, zh = max(sizes["y"] - 1, 1), max(sizes["zh"] - 1, 1)
    everyone = sizes["node"] * sizes["x"] * sizes["core"]

    packed = 3 * half
    piece = packed // everyone
    near = sizes["x"] * sizes["core"]
    ham, cols, start, node_re, node_im, weight_re, weight_im, sweeps = (
        pltpu.with_memory_space_constraint(v, pltpu.HBM)
        for v in (ham, cols, start, node_re, node_im, weight_re, weight_im, sweeps)
    )
    return pl.pallas_call(
        functools.partial(kernel, sizes),
        out_shape=jax.ShapeDtypeStruct((rows, width), F32),
        in_specs=[anywhere] * 8,
        out_specs=pl.BlockSpec(memory_space=pltpu.VMEM),
        scratch_shapes=[
            smem(cols.shape, jnp.int32),
            *[smem(v.shape, F32) for v in (node_re, node_im, weight_re, weight_im)],
            smem(sweeps.shape, jnp.int32),
            vmem(ham.shape, F32),
            vmem((rows, width), F32),
            vmem((2, 2, rows, half), F32),
            vmem((2, rows, half), F32),
            vmem((2, 2, rows, half), F32),
            vmem((3, rows, rows), BF16),
            vmem((3, rows, rows), BF16),
            vmem((8 * (SWEEPS + 1), 128), F32),
            vmem((8 * (SWEEPS + 1), 128), F32),
            vmem((rows, width), BF16),
            vmem((rows, width), BF16),
            dma((8,)),
            dma((3, 2, 2, 2)),
            dma((3, 2, 2, 2)),
            dma((2,)),
            pltpu.SemaphoreType.REGULAR((3,)),
            vmem((packed, half), F32),
            vmem((near, piece, half), F32),
            vmem((piece, half), F32),
            vmem((y, piece, half), F32),
            vmem((piece, half), F32),
            vmem((zh, piece, half), F32),
            vmem((packed, half), F32),
            dma((2, everyone)),
            dma((2, y)),
            dma((2, zh)),
            dma((2, everyone - 1)),
        ],
        compiler_params=pltpu.CompilerParams(collective_id=0, has_side_effects=True, vmem_limit_bytes=40 * 1024 * 1024),
    )(ham, cols, start, node_re, node_im, weight_re, weight_im, sweeps)


def build(finer):
    sizes = dict(finer.shape)
    return jax.shard_map(
        functools.partial(on_device, sizes),
        mesh=finer,
        in_specs=(
            P(ROW, None, None, None),
            P(ROW, None),
            P(ROW, None),
            P("node"),
            P("node"),
            P("node"),
            P("node"),
            P("node"),
        ),
        out_specs=P(ROW, None),
        check_vma=False,
    )


def solution(mesh):
    return build(Mesh(mesh.devices.reshape(mesh.shape["node"], 4, 4, 4, 2), AXES))
```

```python
import functools
import itertools
import math

import jax
import jax.numpy as jnp
from jax import lax
from jax.experimental import pallas as pl
from jax.experimental.pallas import tpu as pltpu
from jax.sharding import Mesh
from jax.sharding import PartitionSpec as P

TILE = 128
REACH = 2
SWEEPS = 2
AXES = ("node", "x", "zh", "y", "core")
ROW = AXES[1:]
MESH = pl.DeviceIdType.MESH
F32 = jnp.float32
BF16 = jnp.bfloat16


def split(value):
    high = value.astype(BF16)
    return high, (value - high.astype(F32)).astype(BF16)


def product(left, right, dims=((1,), (0,))):
    def one(a, b):
        return lax.dot_general(a, b, (dims, ((), ())), preferred_element_type=F32)

    return one(left[0], right[0]) + (one(left[0], right[1]) + one(left[1], right[0]))


def pairwise(values):
    count = len(values)
    if count == 1:
        return values[0]
    if count == 2:
        return values[0] + values[1]
    return (values[0] + values[2]) + (values[1] + values[3])


def steps_over(sizes, axes):
    found = [by for by in itertools.product(*(range(sizes[a]) for a in axes)) if any(by)]
    found.sort(key=lambda by: -sum(min(d, sizes[a] - d) for a, d in zip(axes, by) if a != "core") - 0.1 * by[-1])
    return [dict(zip(axes, by)) for by in found]


class Sum:
    def __init__(self, net, refs):
        self.net = net
        (
            self.part, self.rs_in, self.y_out, self.y_in, self.z_out, self.z_in, self.full,
            self.rs_sem, self.y_sem, self.z_sem, self.ag_sem,
        ) = refs
        self.everyone = steps_over(net.sizes, ("node", "x", "core"))
        self.rows = self.y_out.shape[0]

    def piece(self, at):
        index = 0
        for axis in ("node", "x", "core"):
            index = index * self.net.sizes[axis] + at[axis]
        return pl.ds(pl.multiple_of(index * self.rows, 8), self.rows)

    def partial(self, slot, by):
        peer = self.net.away(**by)
        landing = by["x"] * self.net.sizes["core"] + by["core"]
        return self.net.copy(
            self.part.at[self.piece(peer)],
            self.rs_in.at[landing],
            self.rs_sem.at[0, slot],
            self.rs_sem.at[1, landing],
            peer,
        )

    def scattering(self, by):
        here = jnp.logical_not(self.net.far)
        return here if by["node"] == 0 else here & self.net.edge

    def scatter(self):
        for slot, by in enumerate(self.everyone):

            @pl.when(self.scattering(by))
            def _():
                self.partial(slot, by).start()

    def finish(self):
        for slot, by in enumerate(self.everyone):

            @pl.when(self.scattering(by))
            def _():
                self.partial(slot, by).wait_send()

    def scattered(self):
        ours = self.piece(self.net.me)

        def arrived(landing):
            at = self.rs_in.at[landing]
            self.net.copy(at, at, self.rs_sem.at[0, 0], self.rs_sem.at[1, landing], self.net.away(node=1)).wait_recv()

        @pl.when(self.net.far)
        def _():
            arrived(0)
            self.part[ours, :] = self.rs_in[0]

        value = self.part[ours, :]
        for landing in range(1, self.rs_in.shape[0]):
            arrived(landing)
            value = value + self.rs_in[landing]
        return value

    def order(self, axis):
        size = self.net.sizes[axis]
        return sorted(range(1, size), key=lambda d: -min(d, size - d))

    def share(self, value, axis, source, landing, sem):
        source[...] = value
        self.value = value
        self.landing = landing
        self.copies = [
            self.net.send(source, landing.at[d - 1], sem.at[0, d - 1], sem.at[1, d - 1], self.net.away(**{axis: d}))
            for d in self.order(axis)
        ]

    def shared(self):
        for copy in self.copies:
            copy.wait_recv()
        return pairwise([self.value] + [self.landing[d] for d in range(len(self.copies))])

    def to_z(self):
        self.share(self.scattered(), "zh", self.z_out, self.z_in, self.z_sem)

    def to_y(self):
        self.share(self.shared(), "y", self.y_out, self.y_in, self.y_sem)

    def gather(self):
        value = self.shared()
        ours = self.piece(self.net.me)
        self.full[ours, :] = value
        for slot, by in enumerate(self.everyone):
            self.net.send(
                self.full.at[ours],
                self.full.at[ours],
                self.ag_sem.at[0, slot],
                self.ag_sem.at[1, slot],
                self.net.away(**by),
            )

    def gathered(self):
        for slot, by in enumerate(self.everyone):
            source = self.net.away(**{a: -d for a, d in by.items()})
            theirs = self.full.at[self.piece(source)]
            self.net.copy(
                theirs, theirs, self.ag_sem.at[0, slot], self.ag_sem.at[1, slot], source
            ).wait_recv()


class Net:
    def __init__(self, sizes):
        self.sizes = sizes
        self.me = {a: lax.axis_index(a) for a in AXES}
        self.sent = []
        self.ring = math.prod(sizes[a] for a in ROW)
        me = self.me
        self.position = (
            (me["x"] * sizes["zh"] + me["zh"]) * sizes["y"] + me["y"]
        ) * sizes["core"] + me["core"]
        head = (me["y"] == 0) & (me["core"] == 0)
        tail = (me["y"] == sizes["y"] - 1) & (me["core"] == sizes["core"] - 1)
        self.receives, self.sends = (head, tail), (tail, head)
        self.near = (0, sizes["node"] - 1)
        self.edge = head | tail
        self.filling = (jnp.where(head, 1, 0), jnp.where(head, 0, 1))
        self.far = (head & (me["node"] != self.near[0])) | (tail & (me["node"] != self.near[1]))

    def sending(self, slot):
        return jnp.logical_not(self.sends[slot]) | (self.me["node"] != self.near[slot])

    def target(self, slot):
        node = jnp.where(self.sends[slot], self.near[slot], self.me["node"])
        return {**self.on_ring(1 if slot == 0 else -1), "node": node}

    def relaying(self, slot):
        return self.receives[slot] & (self.me["node"] == self.near[slot])

    def source(self, slot):
        node = jnp.where(self.receives[slot], self.sizes["node"] - 1 - self.near[slot], self.me["node"])
        return {**self.on_ring(-1 if slot == 0 else 1), "node": node}

    def sourced(self, slot):
        return jnp.logical_not(self.receives[slot]) | (self.me["node"] == self.near[slot])

    def away(self, **by):
        return {
            a: lax.rem(self.me[a] + by[a] + self.sizes[a], self.sizes[a]) if by.get(a) else self.me[a]
            for a in AXES
        }

    def on_ring(self, step):
        at = lax.rem(self.position + step + self.ring, self.ring)
        zh, y, core = (self.sizes[a] for a in ("zh", "y", "core"))
        return {
            "node": self.me["node"],
            "x": at // (zh * y * core),
            "zh": lax.rem(at // (y * core), zh),
            "y": lax.rem(at // core, y),
            "core": lax.rem(at, core),
        }

    def copy(self, src, dst, send_sem, recv_sem, peer):
        return pltpu.make_async_remote_copy(
            src_ref=src,
            dst_ref=dst,
            send_sem=send_sem,
            recv_sem=recv_sem,
            device_id=peer,
            device_id_type=MESH,
        )

    def send(self, *what):
        copy = self.copy(*what)
        copy.start()
        self.sent.append(copy)
        return copy


class Halo:
    def __init__(self, net, halo, sem, later=False):
        self.net, self.halo, self.sem, self.later = net, halo, sem, later
        self.tile = halo.shape[2] // 2

    def unit(self, slot, c, j):
        return self.halo.at[slot, c, j * self.tile : (j + 1) * self.tile, :]

    def direct(self, src, slot, c, j):
        return self.net.copy(
            src, self.unit(slot, c, j), self.sem.at[0, slot, c, j], self.sem.at[1, slot, c, j], self.net.target(slot)
        )

    def onward(self, slot, c, j):
        at = self.unit(slot, c, j)
        return self.net.copy(
            at, at, self.sem.at[2, slot, c, j], self.sem.at[1, slot, c, j], self.net.away(node=1)
        )

    def send(self, source, c):
        for slot in range(2):

            @pl.when(self.net.sending(slot))
            def _():
                for j in range(2):
                    self.direct(source(c, j), slot, c, j).start()

    def receive(self, c, slot):
        relaying = ((slot == 0) & self.net.relaying(0)) | ((slot == 1) & self.net.relaying(1))
        for j in range(2):
            self.onward(slot, c, j).wait_recv()

            if not self.later:

                @pl.when(relaying)
                def _():
                    self.onward(slot, c, j).start()

    def relay(self):
        for slot, c, j in itertools.product(range(2), range(2), range(2)):

            @pl.when(self.net.relaying(slot))
            def _():
                self.onward(slot, c, j).start()

    def finish(self):
        for slot in range(2):
            for c, j in itertools.product(range(2), range(2)):

                @pl.when(self.net.sending(slot))
                def _():
                    self.direct(self.unit(slot, c, j), slot, c, j).wait_send()

                @pl.when(self.net.relaying(slot))
                def _():
                    self.onward(slot, c, j).wait_send()


def kernel(
    sizes,
    ham,
    cols_h,
    start,
    node_re_h,
    node_im_h,
    weight_re_h,
    weight_im_h,
    sweeps_h,
    out,
    cols,
    node_re,
    node_im,
    weight_re,
    weight_im,
    sweeps,
    ham_v,
    own,
    halo_v,
    krylov,
    halo1_v,
    band_hi,
    band_lo,
    coef,
    coef_in,
    filt_hi,
    filt_lo,
    local_sem,
    halo_sem,
    halo1_sem,
    coef_sem,
    told,
    *sums,
):
    rows, width = start.shape
    half = width // 2
    net = Net(sizes)
    me, send = net.me, net.send
    position, ring = net.position, net.ring
    twin = net.away(node=1)

    along = [net.away(**{a: d}) for a in ("x", "y", "zh") for d in sorted({1, sizes[a] - 1} - {0})]
    mate = net.away(core=1)
    peers = [mate, twin, *along]
    barrier = pltpu.get_barrier_semaphore()
    greeted = len(peers)
    for slot in range(2):

        @pl.when(net.sourced(slot))
        def _():
            pl.semaphore_signal(barrier, inc=1, device_id=net.source(slot), device_id_type=MESH)

        greeted = greeted + net.sending(slot).astype(jnp.int32)
    for peer in peers:
        pl.semaphore_signal(barrier, inc=1, device_id=peer, device_id_type=MESH)
    ham_copy = pltpu.make_async_copy(ham, ham_v, local_sem.at[0])
    own_copy = pltpu.make_async_copy(start, own, local_sem.at[1])
    few = [
        pltpu.make_async_copy(src, dst, local_sem.at[2 + k])
        for k, (src, dst) in enumerate(
            (
                (cols_h, cols),
                (node_re_h, node_re),
                (node_im_h, node_im),
                (weight_re_h, weight_re),
                (weight_im_h, weight_im),
                (sweeps_h, sweeps),
            )
        )
    ]
    for copy in (*few, ham_copy, own_copy):
        copy.start()
    pl.semaphore_wait(barrier, greeted)

    rounds = (along, [mate, twin], [mate])

    def tell(at):
        for peer in rounds[at]:
            pl.semaphore_signal(told.at[at], inc=1, device_id=peer, device_id_type=MESH)

    def hear(at):
        if rounds[at]:
            pl.semaphore_wait(told.at[at], len(rounds[at]))


    first = Halo(net, halo_v, halo_sem)
    second = Halo(net, halo1_v, halo1_sem, later=True)

    def of_start(c, j):
        return start.at[j * TILE : (j + 1) * TILE, c * half : (c + 1) * half]

    def of_krylov(c, j):
        return krylov.at[c, j * TILE : (j + 1) * TILE, :]

    for c in range(2):
        first.send(of_start, c)
    tell(0)

    for copy in few:
        copy.wait()
    listed = [jnp.zeros((8, 128), F32) for _ in range(SWEEPS + 1)]
    for j in range(node_re.shape[0]):
        re, im = jnp.full((8, 128), node_re[j]), jnp.full((8, 128), node_im[j])
        w_re, w_im = jnp.full((8, 128), weight_re[j]), jnp.full((8, 128), weight_im[j])
        count = jnp.full((8, 128), sweeps[j])
        modulus = re * re + im * im
        inverse_re, inverse_im = re / modulus, -im / modulus
        power_re, power_im = inverse_re, inverse_im
        for degree in range(SWEEPS + 1):
            term = w_re * power_re - w_im * power_im
            listed[degree] = listed[degree] + jnp.where(count >= degree, term, 0.0)
            power_re, power_im = (
                power_re * inverse_re - power_im * inverse_im,
                power_re * inverse_im + power_im * inverse_re,
            )
    for degree, value in enumerate(listed):
        coef[8 * degree : 8 * degree + 8, :] = value
    coef_copy = send(coef, coef_in, coef_sem.at[0], coef_sem.at[1], twin)

    ham_copy.wait()
    mine = rows // TILE
    blocks = mine * ring
    for a in range(mine):
        at = position * mine + a
        offset = [
            lax.rem(cols[a, k] - at + REACH + blocks, blocks) for k in range(ham.shape[1])
        ]
        for p in range(3 * mine):
            o = p - a + REACH - mine
            total = jnp.zeros((TILE, TILE), F32)
            if 0 <= o <= 2 * REACH:
                for k in range(ham.shape[1]):
                    fixed = (REACH, 0, 2 * REACH)
                    if k < 3:
                        if fixed[k] == o:
                            total = total + ham_v[a, k]
                    else:
                        total = total + jnp.where(offset[k] == o, 1.0, 0.0) * ham_v[a, k]
            high, low = split(total)
            side, at_p = p // mine, p % mine
            place = (side, slice(a * TILE, (a + 1) * TILE), slice(at_p * TILE, (at_p + 1) * TILE))
            band_hi[place] = high
            band_lo[place] = low

    def band(side):
        return band_hi[side], band_lo[side]

    own_copy.wait()
    parts = []
    for c in range(2):
        parts.append(product(band(1), split(own[:, c * half : (c + 1) * half])))
    for c in range(2):
        total = parts[c]
        for slot in net.filling:
            first.receive(c, slot)
            total = total + product(band(2 * slot), split(halo_v[slot, c]))
        krylov[c] = total
        second.send(of_krylov, c)
        hear(c)
        tell(c + 1)
    hear(2)
    coef_copy.wait_recv()
    scale = [
        (coef[8 * d : 8 * d + 8, :] + coef_in[8 * d : 8 * d + 8, :])[0:1, 0:1]
        for d in range(SWEEPS + 1)
    ]
    parts = [product(band(1), split(krylov[c])) for c in range(2)]
    packed = Sum(net, sums)

    def filter_rows():
        for c in range(2):
            at = slice(c * half, (c + 1) * half)
            total = parts[c]
            for slot in net.filling:
                second.receive(c, slot)
                total = total + product(band(2 * slot), split(halo1_v[slot, c]))
            total = scale[0] * own[:, at] + scale[1] * krylov[c] + scale[2] * total
            filt_hi[:, at], filt_lo[:, at] = split(total)

    @pl.when(jnp.logical_not(net.far))
    def _():
        filter_rows()
        halves = [
            (filt_hi[:, c * half : (c + 1) * half], filt_lo[:, c * half : (c + 1) * half]) for c in range(2)
        ]
        for k, (a, b) in enumerate(((0, 0), (0, 1), (1, 1))):
            packed.part[k * half : (k + 1) * half, :] = product(halves[a], halves[b], ((0,), (0,)))
    packed.scatter()
    second.relay()
    packed.to_z()
    packed.to_y()
    packed.gather()
    pl.when(net.far)(filter_rows)
    packed.gathered()
    f_split = (filt_hi[...], filt_lo[...])

    corner = packed.full[half : 2 * half, :]
    gram = jnp.concatenate(
        [
            jnp.concatenate([packed.full[0:half, :], corner], axis=1),
            jnp.concatenate([corner.T, packed.full[2 * half :, :]], axis=1),
        ],
        axis=0,
    )
    squares = jnp.sum(jnp.sum(gram * gram, axis=0, keepdims=True), axis=1, keepdims=True)
    norm = jnp.sqrt(squares + 1e-06)
    scale = math.sqrt(rows * ring) / jnp.sqrt(norm)
    by = 1.0 / norm
    g_split = split(gram)
    square = product(g_split, g_split) * (by * by)
    rows_at = lax.broadcasted_iota(jnp.int32, (width, width), 0)
    cols_at = lax.broadcasted_iota(jnp.int32, (width, width), 1)
    diagonal = jnp.where(rows_at == cols_at, 2.25 * scale, 0.0)
    low = diagonal - (2.4375 * scale * by) * gram + (1.6875 * scale) * square
    rest = (0.0625 * scale) * square - (0.5625 * scale * by) * gram
    mixed = low + product(split(square), split(rest))
    out[...] = product(f_split, split(mixed))

    for copy in net.sent:
        copy.wait_send()
    for part in (first, second, packed):
        part.finish()


def on_device(sizes, ham, cols, start, node_re, node_im, weight_re, weight_im, sweeps):
    rows, width = start.shape
    half = width // 2
    anywhere = pl.BlockSpec(memory_space=pl.ANY)
    smem = pltpu.SMEM
    vmem = pltpu.VMEM
    dma = pltpu.SemaphoreType.DMA
    y, zh = max(sizes["y"] - 1, 1), max(sizes["zh"] - 1, 1)
    everyone = sizes["node"] * sizes["x"] * sizes["core"]

    packed = 3 * half
    piece = packed // everyone
    near = sizes["x"] * sizes["core"]
    ham, cols, start, node_re, node_im, weight_re, weight_im, sweeps = (
        pltpu.with_memory_space_constraint(v, pltpu.HBM)
        for v in (ham, cols, start, node_re, node_im, weight_re, weight_im, sweeps)
    )
    return pl.pallas_call(
        functools.partial(kernel, sizes),
        out_shape=jax.ShapeDtypeStruct((rows, width), F32),
        in_specs=[anywhere] * 8,
        out_specs=pl.BlockSpec(memory_space=pltpu.VMEM),
        scratch_shapes=[
            smem(cols.shape, jnp.int32),
            *[smem(v.shape, F32) for v in (node_re, node_im, weight_re, weight_im)],
            smem(sweeps.shape, jnp.int32),
            vmem(ham.shape, F32),
            vmem((rows, width), F32),
            vmem((2, 2, rows, half), F32),
            vmem((2, rows, half), F32),
            vmem((2, 2, rows, half), F32),
            vmem((3, rows, rows), BF16),
            vmem((3, rows, rows), BF16),
            vmem((8 * (SWEEPS + 1), 128), F32),
            vmem((8 * (SWEEPS + 1), 128), F32),
            vmem((rows, width), BF16),
            vmem((rows, width), BF16),
            dma((8,)),
            dma((3, 2, 2, 2)),
            dma((3, 2, 2, 2)),
            dma((2,)),
            pltpu.SemaphoreType.REGULAR((3,)),
            vmem((packed, half), F32),
            vmem((near, piece, half), F32),
            vmem((piece, half), F32),
            vmem((y, piece, half), F32),
            vmem((piece, half), F32),
            vmem((zh, piece, half), F32),
            vmem((packed, half), F32),
            dma((2, everyone)),
            dma((2, y)),
            dma((2, zh)),
            dma((2, everyone - 1)),
        ],
        compiler_params=pltpu.CompilerParams(collective_id=0, has_side_effects=True, vmem_limit_bytes=40 * 1024 * 1024),
    )(ham, cols, start, node_re, node_im, weight_re, weight_im, sweeps)


def build(finer):
    sizes = dict(finer.shape)
    return jax.shard_map(
        functools.partial(on_device, sizes),
        mesh=finer,
        in_specs=(
            P(ROW, None, None, None),
            P(ROW, None),
            P(ROW, None),
            P("node"),
            P("node"),
            P("node"),
            P("node"),
            P("node"),
        ),
        out_specs=P(ROW, None),
        check_vma=False,
    )


def solution(mesh):
    return build(Mesh(mesh.devices.reshape(mesh.shape["node"], 4, 4, 4, 2), AXES))
```

```python
import functools
import itertools
import math

import jax
import jax.numpy as jnp
from jax import lax
from jax.experimental import pallas as pl
from jax.experimental.pallas import tpu as pltpu
from jax.sharding import Mesh
from jax.sharding import PartitionSpec as P

TILE = 128
REACH = 2
SWEEPS = 2
AXES = ("node", "x", "zh", "y", "core")
ROW = AXES[1:]
MESH = pl.DeviceIdType.MESH
F32 = jnp.float32
BF16 = jnp.bfloat16


def split(value):
    high = value.astype(BF16)
    return high, (value - high.astype(F32)).astype(BF16)


def product(left, right, dims=((1,), (0,))):
    def one(a, b):
        return lax.dot_general(a, b, (dims, ((), ())), preferred_element_type=F32)

    return one(left[0], right[0]) + (one(left[0], right[1]) + one(left[1], right[0]))


def pairwise(values):
    count = len(values)
    if count == 1:
        return values[0]
    if count == 2:
        return values[0] + values[1]
    return (values[0] + values[2]) + (values[1] + values[3])


def steps_over(sizes, axes):
    found = [by for by in itertools.product(*(range(sizes[a]) for a in axes)) if any(by)]
    found.sort(key=lambda by: -sum(min(d, sizes[a] - d) for a, d in zip(axes, by) if a != "core") - 0.1 * by[-1])
    return [dict(zip(axes, by)) for by in found]


class Sum:
    def __init__(self, net, refs):
        self.net = net
        (
            self.part, self.rs_in, self.y_out, self.y_in, self.z_out, self.z_in, self.full,
            self.rs_sem, self.y_sem, self.z_sem, self.ag_sem,
        ) = refs
        self.everyone = steps_over(net.sizes, ("node", "x", "core"))
        self.rows = self.y_out.shape[0]

    def piece(self, at):
        index = 0
        for axis in ("node", "x", "core"):
            index = index * self.net.sizes[axis] + at[axis]
        return pl.ds(pl.multiple_of(index * self.rows, 8), self.rows)

    def partial(self, slot, by):
        peer = self.net.away(**by)
        landing = by["x"] * self.net.sizes["core"] + by["core"]
        return self.net.copy(
            self.part.at[self.piece(peer)],
            self.rs_in.at[landing],
            self.rs_sem.at[0, slot],
            self.rs_sem.at[1, landing],
            peer,
        )

    def scattering(self, by):
        here = jnp.logical_not(self.net.far)
        return here if by["node"] == 0 else here & self.net.edge

    def scatter(self):
        for slot, by in enumerate(self.everyone):

            @pl.when(self.scattering(by))
            def _():
                self.partial(slot, by).start()

    def finish(self):
        for slot, by in enumerate(self.everyone):

            @pl.when(self.scattering(by))
            def _():
                self.partial(slot, by).wait_send()

    def scattered(self):
        ours = self.piece(self.net.me)

        def arrived(landing):
            at = self.rs_in.at[landing]
            self.net.copy(at, at, self.rs_sem.at[0, 0], self.rs_sem.at[1, landing], self.net.away(node=1)).wait_recv()

        @pl.when(self.net.far)
        def _():
            arrived(0)
            self.part[ours, :] = self.rs_in[0]

        value = self.part[ours, :]
        for landing in range(1, self.rs_in.shape[0]):
            arrived(landing)
            value = value + self.rs_in[landing]
        return value

    def order(self, axis):
        size = self.net.sizes[axis]
        return sorted(range(1, size), key=lambda d: -min(d, size - d))

    def share(self, value, axis, source, landing, sem):
        source[...] = value
        self.value = value
        self.landing = landing
        self.copies = [
            self.net.send(source, landing.at[d - 1], sem.at[0, d - 1], sem.at[1, d - 1], self.net.away(**{axis: d}))
            for d in self.order(axis)
        ]

    def shared(self):
        for copy in self.copies:
            copy.wait_recv()
        return pairwise([self.value] + [self.landing[d] for d in range(len(self.copies))])

    def to_z(self):
        self.share(self.scattered(), "zh", self.z_out, self.z_in, self.z_sem)

    def to_y(self):
        self.share(self.shared(), "y", self.y_out, self.y_in, self.y_sem)

    def gather(self):
        value = self.shared()
        ours = self.piece(self.net.me)
        self.full[ours, :] = value
        for slot, by in enumerate(self.everyone):
            self.net.send(
                self.full.at[ours],
                self.full.at[ours],
                self.ag_sem.at[0, slot],
                self.ag_sem.at[1, slot],
                self.net.away(**by),
            )

    def gathered(self):
        for slot, by in enumerate(self.everyone):
            source = self.net.away(**{a: -d for a, d in by.items()})
            theirs = self.full.at[self.piece(source)]
            self.net.copy(
                theirs, theirs, self.ag_sem.at[0, slot], self.ag_sem.at[1, slot], source
            ).wait_recv()


class Net:
    def __init__(self, sizes):
        self.sizes = sizes
        self.me = {a: lax.axis_index(a) for a in AXES}
        self.sent = []
        self.ring = math.prod(sizes[a] for a in ROW)
        me = self.me
        self.position = (
            (me["x"] * sizes["zh"] + me["zh"]) * sizes["y"] + me["y"]
        ) * sizes["core"] + me["core"]
        head = (me["y"] == 0) & (me["core"] == 0)
        tail = (me["y"] == sizes["y"] - 1) & (me["core"] == sizes["core"] - 1)
        self.receives, self.sends = (head, tail), (tail, head)
        self.near = (0, sizes["node"] - 1)
        self.edge = head | tail
        self.filling = (jnp.where(head, 1, 0), jnp.where(head, 0, 1))
        self.far = (head & (me["node"] != self.near[0])) | (tail & (me["node"] != self.near[1]))

    def sending(self, slot):
        return jnp.logical_not(self.sends[slot]) | (self.me["node"] != self.near[slot])

    def target(self, slot):
        node = jnp.where(self.sends[slot], self.near[slot], self.me["node"])
        return {**self.on_ring(1 if slot == 0 else -1), "node": node}

    def relaying(self, slot):
        return self.receives[slot] & (self.me["node"] == self.near[slot])

    def source(self, slot):
        node = jnp.where(self.receives[slot], self.sizes["node"] - 1 - self.near[slot], self.me["node"])
        return {**self.on_ring(-1 if slot == 0 else 1), "node": node}

    def sourced(self, slot):
        return jnp.logical_not(self.receives[slot]) | (self.me["node"] == self.near[slot])

    def away(self, **by):
        return {
            a: lax.rem(self.me[a] + by[a] + self.sizes[a], self.sizes[a]) if by.get(a) else self.me[a]
            for a in AXES
        }

    def on_ring(self, step):
        at = lax.rem(self.position + step + self.ring, self.ring)
        zh, y, core = (self.sizes[a] for a in ("zh", "y", "core"))
        return {
            "node": self.me["node"],
            "x": lax.div(at, zh * y * core),
            "zh": lax.rem(lax.div(at, y * core), zh),
            "y": lax.rem(lax.div(at, core), y),
            "core": lax.rem(at, core),
        }

    def copy(self, src, dst, send_sem, recv_sem, peer):
        return pltpu.make_async_remote_copy(
            src_ref=src,
            dst_ref=dst,
            send_sem=send_sem,
            recv_sem=recv_sem,
            device_id=peer,
            device_id_type=MESH,
        )

    def send(self, *what):
        copy = self.copy(*what)
        copy.start()
        self.sent.append(copy)
        return copy


class Halo:
    def __init__(self, net, halo, sem, later=False):
        self.net, self.halo, self.sem, self.later = net, halo, sem, later
        self.tile = halo.shape[2] // 2

    def unit(self, slot, c, j):
        return self.halo.at[slot, c, j * self.tile : (j + 1) * self.tile, :]

    def direct(self, src, slot, c, j):
        return self.net.copy(
            src, self.unit(slot, c, j), self.sem.at[0, slot, c, j], self.sem.at[1, slot, c, j], self.net.target(slot)
        )

    def onward(self, slot, c, j):
        at = self.unit(slot, c, j)
        return self.net.copy(
            at, at, self.sem.at[2, slot, c, j], self.sem.at[1, slot, c, j], self.net.away(node=1)
        )

    def send(self, source, c):
        for slot in range(2):

            @pl.when(self.net.sending(slot))
            def _():
                for j in range(2):
                    self.direct(source(c, j), slot, c, j).start()

    def receive(self, c, slot):
        relaying = ((slot == 0) & self.net.relaying(0)) | ((slot == 1) & self.net.relaying(1))
        for j in range(2):
            self.onward(slot, c, j).wait_recv()

            if not self.later:

                @pl.when(relaying)
                def _():
                    self.onward(slot, c, j).start()

    def relay(self):
        for slot, c, j in itertools.product(range(2), range(2), range(2)):

            @pl.when(self.net.relaying(slot))
            def _():
                self.onward(slot, c, j).start()

    def finish(self):
        for slot in range(2):
            for c, j in itertools.product(range(2), range(2)):

                @pl.when(self.net.sending(slot))
                def _():
                    self.direct(self.unit(slot, c, j), slot, c, j).wait_send()

                @pl.when(self.net.relaying(slot))
                def _():
                    self.onward(slot, c, j).wait_send()


def kernel(
    sizes,
    ham,
    cols_h,
    start,
    node_re_h,
    node_im_h,
    weight_re_h,
    weight_im_h,
    sweeps_h,
    out,
    cols,
    node_re,
    node_im,
    weight_re,
    weight_im,
    sweeps,
    ham_v,
    own,
    halo_v,
    krylov,
    halo1_v,
    band_hi,
    band_lo,
    coef,
    coef_in,
    filt_hi,
    filt_lo,
    local_sem,
    halo_sem,
    halo1_sem,
    coef_sem,
    told,
    *sums,
):
    rows, width = start.shape
    half = width // 2
    net = Net(sizes)
    me, send = net.me, net.send
    position, ring = net.position, net.ring
    twin = net.away(node=1)

    along = [net.away(**{a: d}) for a in ("x", "y", "zh") for d in sorted({1, sizes[a] - 1} - {0})]
    mate = net.away(core=1)
    peers = [mate, twin, *along]
    barrier = pltpu.get_barrier_semaphore()
    greeted = len(peers)
    for slot in range(2):

        @pl.when(net.sourced(slot))
        def _():
            pl.semaphore_signal(barrier, inc=1, device_id=net.source(slot), device_id_type=MESH)

        greeted = greeted + net.sending(slot).astype(jnp.int32)
    for peer in peers:
        pl.semaphore_signal(barrier, inc=1, device_id=peer, device_id_type=MESH)
    ham_copy = pltpu.make_async_copy(ham, ham_v, local_sem.at[0])
    own_copy = pltpu.make_async_copy(start, own, local_sem.at[1])
    few = [
        pltpu.make_async_copy(src, dst, local_sem.at[2 + k])
        for k, (src, dst) in enumerate(
            (
                (cols_h, cols),
                (node_re_h, node_re),
                (node_im_h, node_im),
                (weight_re_h, weight_re),
                (weight_im_h, weight_im),
                (sweeps_h, sweeps),
            )
        )
    ]
    for copy in (*few, ham_copy, own_copy):
        copy.start()
    pl.semaphore_wait(barrier, greeted)

    rounds = (along, [mate, twin], [mate])

    def tell(at):
        for peer in rounds[at]:
            pl.semaphore_signal(told.at[at], inc=1, device_id=peer, device_id_type=MESH)

    def hear(at):
        if rounds[at]:
            pl.semaphore_wait(told.at[at], len(rounds[at]))


    first = Halo(net, halo_v, halo_sem)
    second = Halo(net, halo1_v, halo1_sem, later=True)

    def of_start(c, j):
        return start.at[j * TILE : (j + 1) * TILE, c * half : (c + 1) * half]

    def of_krylov(c, j):
        return krylov.at[c, j * TILE : (j + 1) * TILE, :]

    for c in range(2):
        first.send(of_start, c)
    tell(0)

    for copy in few:
        copy.wait()
    listed = [jnp.zeros((8, 128), F32) for _ in range(SWEEPS + 1)]
    for j in range(node_re.shape[0]):
        re, im = jnp.full((8, 128), node_re[j]), jnp.full((8, 128), node_im[j])
        w_re, w_im = jnp.full((8, 128), weight_re[j]), jnp.full((8, 128), weight_im[j])
        count = jnp.full((8, 128), sweeps[j])
        modulus = re * re + im * im
        inverse_re, inverse_im = re / modulus, -im / modulus
        power_re, power_im = inverse_re, inverse_im
        for degree in range(SWEEPS + 1):
            term = w_re * power_re - w_im * power_im
            listed[degree] = listed[degree] + jnp.where(count >= degree, term, 0.0)
            power_re, power_im = (
                power_re * inverse_re - power_im * inverse_im,
                power_re * inverse_im + power_im * inverse_re,
            )
    for degree, value in enumerate(listed):
        coef[8 * degree : 8 * degree + 8, :] = value
    coef_copy = send(coef, coef_in, coef_sem.at[0], coef_sem.at[1], twin)

    ham_copy.wait()
    mine = rows // TILE
    blocks = mine * ring
    for a in range(mine):
        at = position * mine + a
        offset = [
            lax.rem(cols[a, k] - at + REACH + blocks, blocks) for k in range(ham.shape[1])
        ]
        for p in range(3 * mine):
            o = p - a + REACH - mine
            total = jnp.zeros((TILE, TILE), F32)
            if 0 <= o <= 2 * REACH:
                for k in range(ham.shape[1]):
                    fixed = (REACH, 0, 2 * REACH)
                    if k < 3:
                        if fixed[k] == o:
                            total = total + ham_v[a, k]
                    else:
                        total = total + jnp.where(offset[k] == o, 1.0, 0.0) * ham_v[a, k]
            high, low = split(total)
            side, at_p = p // mine, p % mine
            place = (side, slice(a * TILE, (a + 1) * TILE), slice(at_p * TILE, (at_p + 1) * TILE))
            band_hi[place] = high
            band_lo[place] = low

    def band(side):
        return band_hi[side], band_lo[side]

    own_copy.wait()
    parts = []
    for c in range(2):
        parts.append(product(band(1), split(own[:, c * half : (c + 1) * half])))
    for c in range(2):
        total = parts[c]
        for slot in net.filling:
            first.receive(c, slot)
            total = total + product(band(2 * slot), split(halo_v[slot, c]))
        krylov[c] = total
        second.send(of_krylov, c)
        hear(c)
        tell(c + 1)
    hear(2)
    coef_copy.wait_recv()
    scale = [
        (coef[8 * d : 8 * d + 8, :] + coef_in[8 * d : 8 * d + 8, :])[0:1, 0:1]
        for d in range(SWEEPS + 1)
    ]
    parts = [product(band(1), split(krylov[c])) for c in range(2)]
    packed = Sum(net, sums)

    def filter_rows():
        for c in range(2):
            at = slice(c * half, (c + 1) * half)
            total = parts[c]
            for slot in net.filling:
                second.receive(c, slot)
                total = total + product(band(2 * slot), split(halo1_v[slot, c]))
            total = scale[0] * own[:, at] + scale[1] * krylov[c] + scale[2] * total
            filt_hi[:, at], filt_lo[:, at] = split(total)

    @pl.when(jnp.logical_not(net.far))
    def _():
        filter_rows()
        halves = [
            (filt_hi[:, c * half : (c + 1) * half], filt_lo[:, c * half : (c + 1) * half]) for c in range(2)
        ]
        for k, (a, b) in enumerate(((0, 0), (0, 1), (1, 1))):
            packed.part[k * half : (k + 1) * half, :] = product(halves[a], halves[b], ((0,), (0,)))
    packed.scatter()
    second.relay()
    packed.to_z()
    packed.to_y()
    packed.gather()
    pl.when(net.far)(filter_rows)
    packed.gathered()
    f_split = (filt_hi[...], filt_lo[...])

    corner = packed.full[half : 2 * half, :]
    gram = jnp.concatenate(
        [
            jnp.concatenate([packed.full[0:half, :], corner], axis=1),
            jnp.concatenate([corner.T, packed.full[2 * half :, :]], axis=1),
        ],
        axis=0,
    )
    squares = jnp.sum(jnp.sum(gram * gram, axis=0, keepdims=True), axis=1, keepdims=True)
    norm = jnp.sqrt(squares + 1e-06)
    scale = math.sqrt(rows * ring) / jnp.sqrt(norm)
    by = 1.0 / norm
    g_split = split(gram)
    square = product(g_split, g_split) * (by * by)
    rows_at = lax.broadcasted_iota(jnp.int32, (width, width), 0)
    cols_at = lax.broadcasted_iota(jnp.int32, (width, width), 1)
    diagonal = jnp.where(rows_at == cols_at, 2.25 * scale, 0.0)
    low = diagonal - (2.4375 * scale * by) * gram + (1.6875 * scale) * square
    rest = (0.0625 * scale) * square - (0.5625 * scale * by) * gram
    mixed = low + product(split(square), split(rest))
    out[...] = product(f_split, split(mixed))

    for copy in net.sent:
        copy.wait_send()
    for part in (first, second, packed):
        part.finish()


def on_device(sizes, ham, cols, start, node_re, node_im, weight_re, weight_im, sweeps):
    rows, width = start.shape
    half = width // 2
    anywhere = pl.BlockSpec(memory_space=pl.ANY)
    smem = pltpu.SMEM
    vmem = pltpu.VMEM
    dma = pltpu.SemaphoreType.DMA
    y, zh = max(sizes["y"] - 1, 1), max(sizes["zh"] - 1, 1)
    everyone = sizes["node"] * sizes["x"] * sizes["core"]

    packed = 3 * half
    piece = packed // everyone
    near = sizes["x"] * sizes["core"]
    ham, cols, start, node_re, node_im, weight_re, weight_im, sweeps = (
        pltpu.with_memory_space_constraint(v, pltpu.HBM)
        for v in (ham, cols, start, node_re, node_im, weight_re, weight_im, sweeps)
    )
    return pl.pallas_call(
        functools.partial(kernel, sizes),
        out_shape=jax.ShapeDtypeStruct((rows, width), F32),
        in_specs=[anywhere] * 8,
        out_specs=pl.BlockSpec(memory_space=pltpu.VMEM),
        scratch_shapes=[
            smem(cols.shape, jnp.int32),
            *[smem(v.shape, F32) for v in (node_re, node_im, weight_re, weight_im)],
            smem(sweeps.shape, jnp.int32),
            vmem(ham.shape, F32),
            vmem((rows, width), F32),
            vmem((2, 2, rows, half), F32),
            vmem((2, rows, half), F32),
            vmem((2, 2, rows, half), F32),
            vmem((3, rows, rows), BF16),
            vmem((3, rows, rows), BF16),
            vmem((8 * (SWEEPS + 1), 128), F32),
            vmem((8 * (SWEEPS + 1), 128), F32),
            vmem((rows, width), BF16),
            vmem((rows, width), BF16),
            dma((8,)),
            dma((3, 2, 2, 2)),
            dma((3, 2, 2, 2)),
            dma((2,)),
            pltpu.SemaphoreType.REGULAR((3,)),
            vmem((packed, half), F32),
            vmem((near, piece, half), F32),
            vmem((piece, half), F32),
            vmem((y, piece, half), F32),
            vmem((piece, half), F32),
            vmem((zh, piece, half), F32),
            vmem((packed, half), F32),
            dma((2, everyone)),
            dma((2, y)),
            dma((2, zh)),
            dma((2, everyone - 1)),
        ],
        compiler_params=pltpu.CompilerParams(collective_id=0, has_side_effects=True, vmem_limit_bytes=40 * 1024 * 1024),
    )(ham, cols, start, node_re, node_im, weight_re, weight_im, sweeps)


def build(finer):
    sizes = dict(finer.shape)
    return jax.shard_map(
        functools.partial(on_device, sizes),
        mesh=finer,
        in_specs=(
            P(ROW, None, None, None),
            P(ROW, None),
            P(ROW, None),
            P("node"),
            P("node"),
            P("node"),
            P("node"),
            P("node"),
        ),
        out_specs=P(ROW, None),
        check_vma=False,
    )


def solution(mesh):
    return build(Mesh(mesh.devices.reshape(mesh.shape["node"], 4, 4, 4, 2), AXES))
```
